128 devices in a mesh: seq: 4 (over y_lo, core), blk: 32 (over x, y_hi, z).
Axes of the slice: x: 4, y: 4 (y_hi: 2, y_lo: 2; y = y_hi * 2 + y_lo), z: 4, core: 2. Of those that a mesh axis runs over, the one named last changes fastest.
Arguments:
- tokens: bfloat16 [32768, 8192], P(('seq', 'blk')), may hold values from -21 to 21
- query_weight: bfloat16 [8192, 1024], replicated, may hold values from -0.0625 to 0.0625
- key_weight: bfloat16 [8192, 128], replicated, may hold values from -0.0625 to 0.0625
- value_weight: bfloat16 [8192, 128], replicated, may hold values from -0.0625 to 0.0625
- doc_lengths: int32 [4, 4], replicated, may hold values from 1 to 4096, 8192 in all within a row
- slot_index: int32 [32768], P(('seq', 'blk')), may hold values from 0 to 32767, as said below
Outputs:
- attended: bfloat16 [32768, 1024], P(('seq', 'blk'))
The draws below stay inside these ranges and needn't reach their ends.
Inputs may be any that keep to these rules, and one draw needn't show every extreme that they name: `slot_index`: each value appears exactly once. The 256 rows of one loader device put at most 3 rows into the 256 consecutive slots k * 256 to (k + 1) * 256 - 1 of any k, and exactly 3 into some of them.
All inputs are finite; a program needn't handle non-finite values.
Results may differ from the reference program's by a relative error of at most 0.0085.
The reference program's roundings to bfloat16 on the way count: a program that leaves them out, or rounds other values in their place, can miss the bound.
Values may be sent and summed in bfloat16 or wider, within the bound.
A program may use at most 128 MiB of HBM per device.

```python
import math
import jax
import jax.numpy as jnp
import numpy as np
from jax import lax

D = 8192
HQ = 8
HS = 128
DOCS = 4
TOK_DEV = 256
TOKENS = 32768
GROUP = 8192
LONGEST = 4096
N_SEQ = 4
N_BLK = 32


def draw_tokens(key, part):
    key_values = jax.random.fold_in(key, 0)
    values = jax.random.normal(key_values, (TOKENS, D), jnp.float32)
    return jnp.clip(values, -6.0, 6.0).astype(jnp.bfloat16)


def shuffle_rows(sub_key):
    return jax.random.permutation(sub_key, TOK_DEV).astype(jnp.int32)


def draw_slot_index(key, part):
    device_count = N_SEQ * N_BLK
    base_count = TOK_DEV // device_count
    key_first, key_second, key_recv, key_rows = jax.random.split(key, 4)
    first_shift = jax.random.randint(key_first, (), 0, device_count)
    second_shift = (first_shift + jax.random.randint(key_second, (), 1, device_count)) % device_count
    sender = jnp.arange(device_count, dtype=jnp.int32)[:, None]
    target = jnp.arange(device_count, dtype=jnp.int32)[None, :]
    counts = base_count + (target == (sender + first_shift) % device_count).astype(jnp.int32) - (target == (sender + second_shift) % device_count).astype(jnp.int32)
    ending = jnp.cumsum(counts, axis=1).astype(jnp.int32)
    row_order = jnp.arange(TOK_DEV, dtype=jnp.int32)
    dest_pre = jnp.sum((ending[:, :, None] <= row_order[None, None, :]).astype(jnp.int32), axis=1)
    rank_pre = row_order[None, :] - jnp.take_along_axis(ending - counts, dest_pre, axis=1)
    arrival = (jnp.cumsum(counts, axis=0) - counts).astype(jnp.int32)
    recv_index = jnp.take_along_axis(arrival, dest_pre, axis=1) + rank_pre
    recv_perm = jax.vmap(shuffle_rows)(jax.random.split(key_recv, device_count))
    slot_pre = dest_pre * TOK_DEV + recv_perm[dest_pre, recv_index]
    row_perm = jax.vmap(shuffle_rows)(jax.random.split(key_rows, device_count))
    return jnp.take_along_axis(slot_pre, row_perm, axis=1).reshape(-1).astype(jnp.int32)


def profile(count, total, reach, skew):
    weights = [(1 << 20) // math.isqrt(grade ** skew) + 1 for grade in range(2, count + 1)]
    surplus, given = total - reach - (count - 1), [1] * (count - 1)
    while surplus > 0:
        free = [i for i in range(count - 1) if given[i] < reach]
        whole, budget = sum([weights[i] for i in free]), surplus
        for i in free:
            addition = min(reach - given[i], max(1, budget * weights[i] // whole), surplus)
            given[i] = given[i] + addition
            surplus = surplus - addition
    return np.array([reach] + given)


def ragged(rng, amount, total, bound, skew):
    if amount == 2:
        one = jax.random.randint(rng, (), max(1, total - bound), min(bound, total - 1) + 1)
        return jnp.stack([one, total - one])
    lengths = jnp.asarray(profile(amount, total, bound, skew), jnp.int32)
    twos = (amount - 1) // 2
    giver, receiver = lengths[1:1 + 2 * twos:2], lengths[2:2 + 2 * twos:2]
    room = jnp.minimum(giver - 1, bound - receiver)
    shifted = jax.random.randint(jax.random.fold_in(rng, 1), (twos,), 0, 1 << 20) % (room + 1)
    lengths = lengths.at[1:1 + 2 * twos:2].set(giver - shifted).at[2:2 + 2 * twos:2].set(receiver + shifted)
    return lengths[jax.random.permutation(jax.random.fold_in(rng, 2), amount)]


def gaussian(rng, extent, width, limit, held_as=jnp.bfloat16):
    return jnp.clip(width * jax.random.normal(rng, extent, jnp.float32), -limit, limit).astype(held_as)


def setup_inputs(seed: int = 0) -> dict:
    streams_of = jax.random.split(jax.random.key(seed), 7)
    return {
        "tokens": draw_tokens(jax.random.fold_in(streams_of[6], 71), 0),
        "query_weight": gaussian(streams_of[1], (D, HQ * HS), D ** -0.5, 0.0625),
        "key_weight": gaussian(streams_of[2], (D, HS), D ** -0.5, 0.0625),
        "value_weight": gaussian(streams_of[3], (D, HS), D ** -0.5, 0.0625),
        "doc_lengths": jax.vmap(lambda own: ragged(own, DOCS, GROUP, LONGEST, 2))(jax.random.split(streams_of[4], N_SEQ)).reshape((N_SEQ, DOCS)).astype(jnp.int32),
        "slot_index": draw_slot_index(jax.random.fold_in(streams_of[6], 71), 0),
    }


def rotate_pairs(values, positions):
    half_width = values.shape[-1] // 2
    frequency = 500000.0 ** (-(jnp.arange(half_width, dtype=jnp.float32) * 2.0 / values.shape[-1]))
    angles = positions.astype(jnp.float32)[:, None, None] * frequency[None, None, :]
    cosine = jnp.cos(angles)
    sine_values = jnp.sin(angles)
    leading = values[..., :half_width]
    trailing = values[..., half_width:]
    return jnp.concatenate([leading * cosine - trailing * sine_values, trailing * cosine + leading * sine_values], axis=-1)

def reference(tokens, query_weight, key_weight, value_weight, doc_lengths, slot_index):
    token_count = tokens.shape[0]
    source = jnp.zeros((token_count,), jnp.int32).at[slot_index].set(jnp.arange(token_count, dtype=jnp.int32))
    packed = tokens[source]
    everywhere = jnp.arange(token_count, dtype=jnp.int32)
    local_slot = everywhere % GROUP
    group_index = everywhere // GROUP
    lengths_rows = doc_lengths[group_index]
    doc_ends = jnp.cumsum(lengths_rows, axis=1)
    starts = doc_ends - lengths_rows
    document = lax.optimization_barrier(jnp.sum((local_slot[:, None] >= doc_ends).astype(jnp.int32), axis=1))
    picked = jnp.arange(DOCS, dtype=jnp.int32)[None, :] == document[:, None]
    position = local_slot - lax.optimization_barrier(jnp.sum(jnp.where(picked, starts, 0), axis=1))
    query_f = jnp.dot(packed, query_weight, preferred_element_type=jnp.float32).reshape(token_count, HQ, HS)
    query_rows = rotate_pairs(query_f, position).astype(jnp.bfloat16)
    key_f = jnp.dot(packed, key_weight, preferred_element_type=jnp.float32)
    key_rows = rotate_pairs(key_f[:, None, :], position)[:, 0, :].astype(jnp.bfloat16)
    value_rows = jnp.dot(packed, value_weight, preferred_element_type=jnp.float32).astype(jnp.bfloat16)
    score_scale = 1.0 / math.sqrt(HS)
    block_rows = 512

    def attend(block_number):
        first_row = (block_number * block_rows).astype(jnp.int32)
        group_start = (first_row // GROUP * GROUP).astype(jnp.int32)
        query_block = lax.dynamic_slice_in_dim(query_rows, first_row, block_rows, 0)
        key_block = lax.dynamic_slice_in_dim(key_rows, group_start, GROUP, 0)
        value_block = lax.dynamic_slice_in_dim(value_rows, group_start, GROUP, 0)
        query_doc = lax.dynamic_slice_in_dim(document, first_row, block_rows, 0)
        key_doc = lax.dynamic_slice_in_dim(document, group_start, GROUP, 0)
        query_local = lax.dynamic_slice_in_dim(local_slot, first_row, block_rows, 0)
        key_local = lax.dynamic_slice_in_dim(local_slot, group_start, GROUP, 0)
        allowed = (query_doc[:, None] == key_doc[None, :]) & (key_local[None, :] <= query_local[:, None])
        allowed = allowed[:, None, :]
        scores = jnp.einsum('qhd,kd->qhk', query_block.astype(jnp.float32), key_block.astype(jnp.float32)) * score_scale
        scores = jnp.where(allowed, scores, -1e+30)
        row_max = lax.optimization_barrier(jnp.max(scores, axis=-1, keepdims=True))
        weights = jnp.where(allowed, jnp.exp(scores - row_max), 0.0)
        denominator = lax.optimization_barrier(jnp.sum(weights, axis=-1))
        rounded = weights.astype(jnp.bfloat16)
        numerator = jnp.einsum('qhk,kd->qhd', rounded.astype(jnp.float32), value_block.astype(jnp.float32))
        return (numerator / denominator[..., None]).astype(jnp.bfloat16).reshape(block_rows, HQ * HS)
    blocks = lax.map(attend, jnp.arange(token_count // block_rows, dtype=jnp.int32))
    packed_out = blocks.reshape(token_count, HQ * HS)
    return packed_out[slot_index]
```

```python
import functools
import math

import jax
import jax.numpy as jnp
from jax import lax
from jax.experimental import pallas as pl
from jax.experimental.pallas import tpu as pltpu
from jax.sharding import PartitionSpec as P

HQ = 8
HS = 128
D = 8192
ROWS = 256
NBLOCKS = 32
CAP = 3
PACK = 48
NPACK = 8 * PACK
QW = 128 + HQ * HS
KT = 512
CHUNK = 32
NCHUNK = NPACK // CHUNK
MESH = pl.DeviceIdType.MESH
BF = jnp.bfloat16
F32 = jnp.float32
HIGHEST = lax.Precision.HIGHEST


def place():
    seq = lax.axis_index("seq")
    blk = lax.axis_index("blk")
    core = seq % 2
    y = (blk // 4) % 2 * 2 + seq // 2
    return blk // 8, y, blk % 4, core


def device(x, y, z, c):
    return ((y % 2) * 2 + c, (x * 2 + y // 2) * 4 + z)


def block_id(x, y, c):
    return c * 16 + x * 4 + y


def dot_t(a, b):
    return lax.dot_general(a, b, (((0,), (0,)), ((), ())), preferred_element_type=F32)


def rope(v, cos, sin):
    return v * cos + pltpu.roll(v, HS // 2, 1) * sin


def front_kernel(
    tok, wq, wk, wv, cos, sin, meta, pidx,
    qin, kall, vtall,
    tok_v, wkv_v, wq_v, acc, kvs, zin, perm, aout, ain, kblk, vblk, qs,
    tok_sem, wq_sem, zs_sem, zr_sem, as_sem, ar_sem, qs_sem, qr_sem,
    ts_sem, tr_sem, ds_sem, dr_sem, loc_sem,
):
    x, y, z, c = place()
    kc = D // 4
    mine = block_id(x, y, c)
    line = z * 2 + c

    loads = []
    for i in range(4):
        part = pl.ds(i * kc, kc)
        loads.append([
            pltpu.make_async_copy(tok.at[:, part], tok_v.at[:, part], tok_sem.at[0, i]),
            pltpu.make_async_copy(wk.at[part, :], wkv_v.at[part, pl.ds(0, HS)], tok_sem.at[1, i]),
            pltpu.make_async_copy(wv.at[part, :], wkv_v.at[part, pl.ds(HS, HS)], tok_sem.at[2, i]),
        ])
        for load in loads[i]:
            load.start()
    qloads = []
    for n in range(4):
        cols = pl.ds(n * 256, 256)
        qloads.append(pltpu.make_async_copy(wq.at[:, cols], wq_v.at[n], wq_sem.at[n]))
        qloads[n].start()

    peers = []
    for dz in range(4):
        for dc in range(2):
            if (dz, dc) != (0, 0):
                peers.append(((z + dz) % 4, (c + dc) % 2))
    flat = []
    for dx in range(4):
        for dy in range(4):
            for dc in range(2):
                if (dx, dy, dc) != (0, 0, 0):
                    flat.append(((x + dx) % 4, (y + dy) % 4, (c + dc) % 2))
    barrier = pltpu.get_barrier_semaphore()
    for pz, pc in peers:
        pl.semaphore_signal(barrier, inc=1, device_id=device(x, y, pz, pc), device_id_type=MESH)
    for px, py, pc in flat:
        if True:
            pl.semaphore_signal(barrier, inc=1, device_id=device(px, py, z, pc), device_id_type=MESH)

    lane = lax.broadcasted_iota(jnp.int32, (NPACK, ROWS), 0)
    pack = (lane == pidx[...]).astype(F32).astype(BF)
    row = lax.broadcasted_iota(jnp.int32, (512, NPACK), 0)
    col = lax.broadcasted_iota(jnp.int32, (512, NPACK), 1)
    j = row >> 4
    slot12 = row & 15
    zz = (slot12 >= 3).astype(jnp.int32) + (slot12 >= 6).astype(jnp.int32) + (slot12 >= 9).astype(jnp.int32)
    source = zz * 96 + (j & 1) * 48 + (j >> 1) * 3 + (slot12 - 3 * zz)
    perm[...] = ((source == col) & (slot12 < 12)).astype(F32).astype(BF)

    for i in range(4):
        part = pl.ds(i * kc, kc)
        for load in loads[i]:
            load.wait()
        product = jnp.dot(tok_v[:, part], wkv_v[part, :], preferred_element_type=F32)
        if i == 0:
            acc[...] = product
        else:
            acc[...] += product
    k_rows = rope(acc[:, :HS], cos[...], sin[...]).astype(BF)
    v_rows = acc[:, HS:].astype(BF)
    kvs[:, 0:HS] = jnp.dot(pack, k_rows, preferred_element_type=F32).astype(BF)
    kvs[:, HS:2 * HS] = jnp.dot(pack, v_rows, preferred_element_type=F32).astype(BF)
    slots = jnp.dot(pack, meta[...], preferred_element_type=F32).astype(BF)
    kvs[:, 2 * HS:] = slots
    qs[:, 0:128] = slots

    pl.semaphore_wait(barrier, 7 + 31)

    sends = []
    for dz in range(1, 4):
        pz = (z + dz) % 4
        sends.append(pltpu.make_async_remote_copy(
            src_ref=kvs.at[pl.ds(pz * 96, 96), :], dst_ref=zin.at[pl.ds(z * 96, 96), :],
            send_sem=zs_sem.at[dz - 1], recv_sem=zr_sem.at[0],
            device_id=device(x, y, pz, c), device_id_type=MESH))
        sends[-1].start()
    pltpu.make_async_copy(
        kvs.at[pl.ds(z * 96, 96), :], zin.at[pl.ds(z * 96, 96), :], zr_sem.at[0]).start()

    def query_block(n):
        qloads[n].wait()

        def step(i, total):
            part = pl.ds(pl.multiple_of(i * kc, kc), kc)
            return total + jnp.dot(tok_v[:, part], wq_v[n, part, :], preferred_element_type=F32)

        acc[...] = jnp.zeros_like(acc)

        @pl.loop(0, 4)
        def _(i):
            part = pl.ds(pl.multiple_of(i * kc, kc), kc)
            acc[...] += jnp.dot(tok_v[:, part], wq_v[n, part, :], preferred_element_type=F32)

        for h in range(2):
            rows = rope(acc[:, h * HS:(h + 1) * HS], cos[...], sin[...]).astype(BF)
            at = 128 + (n * 2 + h) * HS
            qs[:, at:at + HS] = jnp.dot(pack, rows, preferred_element_type=F32).astype(BF)

    def query_send(half):
        cols = pl.ds(0, 640) if half == 0 else pl.ds(640, 512)
        for i, (pz, pc) in enumerate(peers):
            sends.append(pltpu.make_async_remote_copy(
                src_ref=qs.at[pl.ds((pz * 2 + pc) * PACK, PACK), cols],
                dst_ref=qin.at[pl.ds(line * PACK, PACK), cols],
                send_sem=qs_sem.at[half, i], recv_sem=qr_sem.at[0],
                device_id=device(x, y, pz, pc), device_id_type=MESH))
            sends[-1].start()
        pltpu.make_async_copy(
            qs.at[pl.ds(line * PACK, PACK), cols], qin.at[pl.ds(line * PACK, PACK), cols],
            qr_sem.at[0]).start()

    query_block(0)

    pltpu.make_async_copy(zin, zin, zr_sem.at[0]).wait()
    aout[...] = jnp.dot(perm[...], zin[...], preferred_element_type=F32).astype(BF)
    for i, (px, py, pc) in enumerate(flat):
        sends.append(pltpu.make_async_remote_copy(
            src_ref=aout.at[pl.ds(block_id(px, py, pc) * 16, 16), :],
            dst_ref=ain.at[pl.ds(mine * 16, 16), :],
            send_sem=as_sem.at[i], recv_sem=ar_sem.at[0],
            device_id=device(px, py, z, pc), device_id_type=MESH))
        sends[-1].start()
    pltpu.make_async_copy(
        aout.at[pl.ds(mine * 16, 16), :], ain.at[pl.ds(mine * 16, 16), :], ar_sem.at[0]).start()

    query_block(1)
    query_send(0)

    pltpu.make_async_copy(ain, ain, ar_sem.at[0]).wait()
    got = ain[:, 2 * HS:].astype(F32)
    want = (lax.broadcasted_iota(jnp.int32, (512, HS), 1) + 1).astype(F32)
    one = jnp.concatenate([
        (got == want).astype(F32), (got == want + 128.0).astype(F32)], axis=1).astype(BF)
    kblk[...] = dot_t(one, ain[:, 0:HS]).astype(BF)
    vblk[...] = dot_t(ain[:, HS:2 * HS], one).astype(BF)

    def where(o):
        return block_id((x + o[0]) % 4, (y + o[1]) % 4, c)

    def piece(q, o):
        if q < 2:
            return kall.at[where(o), pl.ds(q * 128, 128), :]
        return vtall.at[where(o), pl.ds((q - 2) * 64, 64), :]

    def own(q):
        if q < 2:
            return kblk.at[pl.ds(q * 128, 128), :]
        return vblk.at[pl.ds((q - 2) * 64, 64), :]

    count = [0]

    def push(q, o, step):
        e = ((step[0]) % 4, (step[1]) % 4)
        rel = ((o[0] - e[0]) % 4, (o[1] - e[1]) % 4)
        src = own(q) if o == (0, 0) else piece(q, o)
        sends.append(pltpu.make_async_remote_copy(
            src_ref=src, dst_ref=piece(q, o),
            send_sem=ts_sem.at[count[0]], recv_sem=tr_sem.at[q * 16 + rel[0] * 4 + rel[1]],
            device_id=device((x + e[0]) % 4, (y + e[1]) % 4, z, c), device_id_type=MESH))
        sends[-1].start()
        count[0] += 1

    def share(q, o):
        src = own(q) if o == (0, 0) else piece(q, o)
        sends.append(pltpu.make_async_remote_copy(
            src_ref=src, dst_ref=piece(q, o),
            send_sem=ds_sem.at[q * 16 + o[0] * 4 + o[1]], recv_sem=dr_sem.at[0 if q < 2 else 1],
            device_id=device(x, y, z, 1 - c), device_id_type=MESH))
        sends[-1].start()

    def axes(q):
        return ((1, 0), (0, 1)) if q < 2 else ((0, 1), (1, 0))

    def offset(q, a, b):
        first, second = axes(q)
        return ((a * first[0] + b * second[0]) % 4, (a * first[1] + b * second[1]) % 4)

    def scaled(v, d):
        return (v[0] * d, v[1] * d)

    def forward(q, a, b):
        first, second = axes(q)
        d = 1 if q % 2 == 0 else -1
        o = offset(q, a, b)
        if b == 0:
            if a == 0:
                push(q, o, scaled(first, 1))
                push(q, o, scaled(first, -1))
            elif a == (-d) % 4:
                push(q, o, scaled(first, d))
            push(q, o, scaled(second, 1))
            push(q, o, scaled(second, -1))
        elif b == (-d) % 4:
            push(q, o, scaled(second, d))
        share(q, o)

    local = []
    for q in range(4):
        local.append(pltpu.make_async_copy(own(q), piece(q, (0, 0)), loc_sem.at[q]))
        local[-1].start()
        forward(q, 0, 0)

    query_block(2)

    def arrive(q, a, b):
        o = offset(q, a, b)
        ref = piece(q, o)
        pltpu.make_async_copy(ref, ref, tr_sem.at[q * 16 + o[0] * 4 + o[1]]).wait()
        forward(q, a, b)

    for a, b in ((1, 0), (3, 0), (0, 1), (0, 3)):
        for q in range(4):
            arrive(q, a, b)

    query_block(3)
    query_send(1)

    for a, b in ((2, 0), (1, 1), (1, 3), (3, 1), (3, 3), (0, 2), (2, 1), (2, 3), (1, 2), (3, 2), (2, 2)):
        for q in range(4):
            arrive(q, a, b)

    other = pl.ds((1 - c) * 16, 16)
    pltpu.make_async_copy(kall.at[other], kall.at[other], dr_sem.at[0]).wait()
    pltpu.make_async_copy(vtall.at[other], vtall.at[other], dr_sem.at[1]).wait()
    pltpu.make_async_copy(qin, qin, qr_sem.at[0]).wait()
    for copy in local:
        copy.wait()
    for copy in sends:
        copy.wait_send()


def front(tokens, wq, wk, wv, cos, sin, meta, pidx):
    anyspace = pl.BlockSpec(memory_space=pl.ANY)
    vmem = pl.BlockSpec(memory_space=pltpu.VMEM)
    dma = pltpu.SemaphoreType.DMA
    return pl.pallas_call(
        front_kernel,
        out_shape=(
            jax.ShapeDtypeStruct((NPACK, QW), BF),
            jax.ShapeDtypeStruct((NBLOCKS, ROWS, HS), BF),
            jax.ShapeDtypeStruct((NBLOCKS, HS, ROWS), BF),
        ),
        in_specs=[anyspace] * 4 + [vmem] * 4,
        out_specs=(anyspace, anyspace, anyspace),
        scratch_shapes=[
            pltpu.VMEM((ROWS, D), BF),
            pltpu.VMEM((D, 2 * HS), BF),
            pltpu.VMEM((4, D, 256), BF),
            pltpu.VMEM((ROWS, 256), F32),
            pltpu.VMEM((NPACK, 3 * HS), BF),
            pltpu.VMEM((NPACK, 3 * HS), BF),
            pltpu.VMEM((512, NPACK), BF),
            pltpu.VMEM((512, 3 * HS), BF),
            pltpu.VMEM((512, 3 * HS), BF),
            pltpu.VMEM((ROWS, HS), BF),
            pltpu.VMEM((HS, ROWS), BF),
            pltpu.VMEM((NPACK, QW), BF),
            dma((3, 4)), dma((4,)), dma((3,)), dma((1,)), dma((31,)), dma((1,)),
            dma((2, 7)), dma((1,)), dma((60,)), dma((64,)), dma((64,)), dma((2,)), dma((4,)),
        ],
        compiler_params=pltpu.CompilerParams(
            collective_id=0, has_side_effects=True, vmem_limit_bytes=50 << 20),
        name="front",
    )(tokens, wq, wk, wv, cos, sin, meta, pidx)


def attend_kernel(ends, qin, kall, vtall, out, rank_s, slot_s, one_s, qsort, osort):
    c = ends[4]
    shape = (NPACK, HS)
    i = lax.broadcasted_iota(jnp.int32, shape, 0)
    w = i - ((i * 43691) >> 21) * PACK
    base = ((w * 43691) >> 17) * 2 + c
    m = qin[:, 0:HS].astype(F32)
    slot = jnp.where(m > 0.0, base.astype(F32) * 256.0 + m - 1.0, 8192.0 + i.astype(F32))
    slot_row = jnp.transpose(slot)[0:1, :]
    slot_wide = jnp.concatenate([slot] * 3, axis=1)
    rank = jnp.sum((slot_row < slot_wide).astype(F32), axis=1, keepdims=True)
    lane = lax.broadcasted_iota(jnp.int32, (NPACK, NPACK), 1).astype(F32)
    one = (lane == rank).astype(F32)
    one_s[...] = one.astype(BF)
    rank_s[...] = jnp.broadcast_to(rank, shape)
    slot_s[...] = slot
    qsort[...] = dot_t(one_s[...], qin[:, HS:]).astype(BF)
    osort[...] = jnp.zeros_like(osort)
    scale = math.log2(math.e) / math.sqrt(HS)
    wide = CHUNK * HQ

    def chunk(n, carry):
        lane_q = (lax.broadcasted_iota(jnp.int32, (NPACK, HS), 1) & (CHUNK - 1)) + n * CHUNK
        pick = rank_s[...] == lane_q.astype(F32)
        half = jnp.sum(jnp.where(pick, slot_s[...], 0.0), axis=0, keepdims=True)
        mine = jnp.concatenate([half, half], axis=1).astype(jnp.int32)
        start = jnp.zeros_like(mine)
        for d in range(3):
            start = jnp.where(mine >= ends[d], ends[d], start)
        low = jnp.min(start)
        high = jnp.max(jnp.where(mine < 8192, mine, -1))

        @pl.when(high >= 0)
        def _():
            rows = pl.ds(pl.multiple_of(n * CHUNK, CHUNK), CHUNK)
            queries = jnp.concatenate(
                [qsort[rows, h * HS:(h + 1) * HS] for h in range(HQ)], axis=0)

            def tile(t, state):
                top, total, acc = state
                keys = kall[pl.ds(pl.multiple_of(t * KT, KT), KT), :]
                s = lax.dot_general(keys, queries, (((1,), (1,)), ((), ())), preferred_element_type=F32)
                at = lax.broadcasted_iota(jnp.int32, (KT, wide), 0) + t * KT
                allowed = (at >= start) & (at <= mine)
                s = jnp.where(allowed, s, -1e30)
                new = jnp.maximum(top, jnp.max(s, axis=0, keepdims=True))
                p = jnp.exp2((s - new) * scale)
                factor = jnp.exp2((top - new) * scale)
                total = total * factor + jnp.sum(p, axis=0, keepdims=True)
                pb = p.astype(BF)
                acc = acc * factor
                for u in range(KT // ROWS):
                    acc = acc + jnp.dot(
                        vtall[t * (KT // ROWS) + u], pb[u * ROWS:(u + 1) * ROWS, :],
                        preferred_element_type=F32)
                return new, total, acc

            state = (
                jnp.full((1, wide), -1e30, F32), jnp.zeros((1, wide), F32), jnp.zeros((HS, wide), F32))
            top, total, acc = lax.fori_loop(low // KT, high // KT + 1, tile, state)
            o = jnp.transpose(acc / total).astype(BF)
            for h in range(HQ):
                osort[rows, h * HS:(h + 1) * HS] = o[h * CHUNK:(h + 1) * CHUNK, :]

        return carry

    lax.fori_loop(0, NCHUNK, chunk, 0)
    out[...] = jnp.dot(one_s[...], osort[...], preferred_element_type=F32).astype(BF)


def attend(ends, qin, kall, vtall):
    vmem = pl.BlockSpec(memory_space=pltpu.VMEM)
    return pl.pallas_call(
        attend_kernel,
        out_shape=jax.ShapeDtypeStruct((NPACK, HQ * HS), BF),
        in_specs=[pl.BlockSpec(memory_space=pltpu.SMEM), vmem, vmem, vmem],
        out_specs=vmem,
        scratch_shapes=[
            pltpu.VMEM((NPACK, HS), F32),
            pltpu.VMEM((NPACK, HS), F32),
            pltpu.VMEM((NPACK, NPACK), BF),
            pltpu.VMEM((NPACK, HQ * HS), BF),
            pltpu.VMEM((NPACK, HQ * HS), BF),
        ],
        compiler_params=pltpu.CompilerParams(vmem_limit_bytes=40 << 20),
        name="attend",
    )(ends, qin, kall.reshape(NBLOCKS * ROWS, HS), vtall)


def back_kernel(packed, ret, send_sem, recv_sem):
    x, y, z, c = place()
    line = z * 2 + c
    peers = []
    for dz in range(4):
        for dc in range(2):
            if (dz, dc) != (0, 0):
                peers.append(((z + dz) % 4, (c + dc) % 2))
    barrier = pltpu.get_barrier_semaphore()
    for pz, pc in peers:
        pl.semaphore_signal(barrier, inc=1, device_id=device(x, y, pz, pc), device_id_type=MESH)
    pl.semaphore_wait(barrier, 7)
    sends = []
    for i, (pz, pc) in enumerate(peers):
        sends.append(pltpu.make_async_remote_copy(
            src_ref=packed.at[pl.ds((pz * 2 + pc) * PACK, PACK), :],
            dst_ref=ret.at[pl.ds(line * PACK, PACK), :],
            send_sem=send_sem.at[i], recv_sem=recv_sem.at[0],
            device_id=device(x, y, pz, pc), device_id_type=MESH))
        sends[-1].start()
    pltpu.make_async_copy(
        packed.at[pl.ds(line * PACK, PACK), :], ret.at[pl.ds(line * PACK, PACK), :], recv_sem.at[0]).start()
    pltpu.make_async_copy(ret, ret, recv_sem.at[0]).wait()
    for copy in sends:
        copy.wait_send()


def back(packed):
    anyspace = pl.BlockSpec(memory_space=pl.ANY)
    return pl.pallas_call(
        back_kernel,
        out_shape=jax.ShapeDtypeStruct((NPACK, HQ * HS), BF),
        in_specs=[anyspace],
        out_specs=anyspace,
        scratch_shapes=[pltpu.SemaphoreType.DMA((7,)), pltpu.SemaphoreType.DMA((1,))],
        compiler_params=pltpu.CompilerParams(collective_id=1, has_side_effects=True),
        name="back",
    )(packed)


def shards(tokens, query_weight, key_weight, value_weight, doc_lengths, slot_index):
    x, y, z, c = place()
    order = jnp.arange(ROWS, dtype=jnp.int32)
    block = slot_index // ROWS
    same = block[:, None] == block[None, :]
    rank = jnp.sum((same & (order[None, :] < order[:, None])).astype(jnp.int32), axis=1)
    group = block // NBLOCKS
    local_block = block % NBLOCKS
    pidx = group * 96 + (local_block % 2) * PACK + (local_block // 2) * CAP + rank
    local = slot_index % (NBLOCKS * ROWS)
    ends = jnp.cumsum(doc_lengths, axis=1)
    in_group = group[:, None] == jnp.arange(4, dtype=jnp.int32)[None, :]
    start = jnp.zeros_like(local)
    for d in range(3):
        end = jnp.sum(jnp.where(in_group, ends[:, d][None, :], 0), axis=1)
        start = jnp.where(local >= end, end, start)
    position = local - start
    frequency = 500000.0 ** (-(jnp.arange(HS // 2, dtype=F32) * 2.0 / HS))
    angles = position.astype(F32)[:, None] * frequency[None, :]
    cosine = jnp.cos(angles)
    sine = jnp.sin(angles)
    cos = jnp.concatenate([cosine, cosine], axis=1)
    sin = jnp.concatenate([-sine, sine], axis=1)
    meta = jnp.broadcast_to((slot_index % ROWS + 1).astype(BF)[:, None], (ROWS, HS))
    qin, kall, vtall = front(
        tokens, query_weight, key_weight, value_weight, cos, sin, meta, pidx[None, :])
    mine = jnp.sum(jnp.where(jnp.arange(4)[:, None] == z, ends, 0), axis=0)
    scalars = jnp.concatenate([mine, c[None], jnp.zeros((3,), jnp.int32)]).astype(jnp.int32)
    packed = attend(scalars, qin, kall, vtall)
    returned = back(packed)
    pick = (pidx[:, None] == jnp.arange(NPACK, dtype=jnp.int32)[None, :]).astype(BF)
    return jnp.dot(pick, returned, preferred_element_type=F32).astype(BF)


def solution(mesh):
    in_specs = (P(("seq", "blk"), None), P(), P(), P(), P(), P(("seq", "blk")))
    out_specs = P(("seq", "blk"), None)
    return jax.shard_map(shards, mesh=mesh, in_specs=in_specs, out_specs=out_specs, check_vma=False)
```

```python
import functools
import math

import jax
import jax.numpy as jnp
from jax import lax
from jax.experimental import pallas as pl
from jax.experimental.pallas import tpu as pltpu
from jax.sharding import PartitionSpec as P

HQ = 8
HS = 128
D = 8192
ROWS = 256
NBLOCKS = 32
CAP = 3
PACK = 48
NPACK = 8 * PACK
QW = 128 + HQ * HS
KT = 512
KPARTS = 8
CHUNK = 32
NCHUNK = NPACK // CHUNK
MESH = pl.DeviceIdType.MESH
BF = jnp.bfloat16
F32 = jnp.float32
HIGHEST = lax.Precision.HIGHEST


def place():
    seq = lax.axis_index("seq")
    blk = lax.axis_index("blk")
    core = seq % 2
    y = (blk // 4) % 2 * 2 + seq // 2
    return blk // 8, y, blk % 4, core


def device(x, y, z, c):
    return ((y % 2) * 2 + c, (x * 2 + y // 2) * 4 + z)


def block_id(x, y, c):
    return c * 16 + x * 4 + y


def dot_t(a, b):
    return lax.dot_general(a, b, (((0,), (0,)), ((), ())), preferred_element_type=F32)


def rope(v, cos, sin):
    return v * cos + pltpu.roll(v, HS // 2, 1) * sin


def starts(slots, ends):
    start = jnp.zeros_like(slots)
    for d in range(3):
        start = jnp.where(slots >= ends[d], ends[d], start)
    return start


def front_kernel(
    ends, tok, wq, wk, wv, cos, sin, meta, pidx,
    kall, vtall, qsort, one_o, lanes_o, bounds_o,
    tok_v, wkv_v, wq_v, acc, kvs, zin, perm, aout, ain, kblk, vblk, qs, qin,
    tok_sem, wq_sem, zs_sem, zr_sem, as_sem, ar_sem, qs_sem, qr_sem,
    ts_sem, tr_sem, ds_sem, dr_sem, loc_sem,
):
    x, y, z, c = place()
    kc = D // KPARTS
    mine = block_id(x, y, c)
    line = z * 2 + c

    loads = []
    for i in range(KPARTS):
        part = pl.ds(i * kc, kc)
        loads.append([
            pltpu.make_async_copy(tok.at[:, part], tok_v.at[:, part], tok_sem.at[0, i]),
            pltpu.make_async_copy(wk.at[part, :], wkv_v.at[part, pl.ds(0, HS)], tok_sem.at[1, i]),
            pltpu.make_async_copy(wv.at[part, :], wkv_v.at[part, pl.ds(HS, HS)], tok_sem.at[2, i]),
        ])
        for load in loads[i]:
            load.start()
    qloads = []
    for n in range(4):
        cols = pl.ds(n * 256, 256)
        qloads.append(pltpu.make_async_copy(wq.at[:, cols], wq_v.at[n], wq_sem.at[n]))

    peers = []
    for dz in range(4):
        for dc in range(2):
            if (dz, dc) != (0, 0):
                peers.append(((z + dz) % 4, (c + dc) % 2))
    flat = []
    for dx in range(4):
        for dy in range(4):
            for dc in range(2):
                if (dx, dy, dc) != (0, 0, 0):
                    flat.append(((x + dx) % 4, (y + dy) % 4, (c + dc) % 2))
    barrier = pltpu.get_barrier_semaphore()
    for pz, pc in peers:
        pl.semaphore_signal(barrier, inc=1, device_id=device(x, y, pz, pc), device_id_type=MESH)
    for px, py, pc in flat:
        pl.semaphore_signal(barrier, inc=1, device_id=device(px, py, z, pc), device_id_type=MESH)

    lane = lax.broadcasted_iota(jnp.int32, (NPACK, ROWS), 0)
    pack = (lane == pidx[...]).astype(F32).astype(BF)
    row = lax.broadcasted_iota(jnp.int32, (512, NPACK), 0)
    col = lax.broadcasted_iota(jnp.int32, (512, NPACK), 1)
    j = row >> 4
    slot12 = row & 15
    zz = (slot12 >= 3).astype(jnp.int32) + (slot12 >= 6).astype(jnp.int32) + (slot12 >= 9).astype(jnp.int32)
    source = zz * 96 + (j & 1) * 48 + (j >> 1) * 3 + (slot12 - 3 * zz)
    perm[...] = ((source == col) & (slot12 < 12)).astype(F32).astype(BF)
    slots = jnp.dot(pack, meta[...], preferred_element_type=F32).astype(BF)
    kvs[:, 2 * HS:] = slots
    qs[:, 0:128] = slots

    for i in range(KPARTS):
        part = pl.ds(i * kc, kc)
        for load in loads[i]:
            load.wait()
        product = jnp.dot(tok_v[:, part], wkv_v[part, :], preferred_element_type=F32)
        if i == 0:
            acc[...] = product
        else:
            acc[...] += product
    for load in qloads:
        load.start()
    k_rows = rope(acc[:, :HS], cos[...], sin[...]).astype(BF)
    v_rows = acc[:, HS:].astype(BF)
    kvs[:, 0:HS] = jnp.dot(pack, k_rows, preferred_element_type=F32).astype(BF)
    kvs[:, HS:2 * HS] = jnp.dot(pack, v_rows, preferred_element_type=F32).astype(BF)

    pl.semaphore_wait(barrier, 7 + 31)

    sends = []
    for dz in range(1, 4):
        pz = (z + dz) % 4
        sends.append(pltpu.make_async_remote_copy(
            src_ref=kvs.at[pl.ds(pz * 96, 96), :], dst_ref=zin.at[pl.ds(z * 96, 96), :],
            send_sem=zs_sem.at[dz - 1], recv_sem=zr_sem.at[0],
            device_id=device(x, y, pz, c), device_id_type=MESH))
        sends[-1].start()
    pltpu.make_async_copy(
        kvs.at[pl.ds(z * 96, 96), :], zin.at[pl.ds(z * 96, 96), :], zr_sem.at[0]).start()

    def query_block(n):
        qloads[n].wait()
        acc[...] = jnp.zeros_like(acc)

        @pl.loop(0, 4)
        def _(i):
            part = pl.ds(pl.multiple_of(i * (D // 4), D // 4), D // 4)
            acc[...] += jnp.dot(tok_v[:, part], wq_v[n, part, :], preferred_element_type=F32)

        for h in range(2):
            rows = rope(acc[:, h * HS:(h + 1) * HS], cos[...], sin[...]).astype(BF)
            at = 128 + (n * 2 + h) * HS
            qs[:, at:at + HS] = jnp.dot(pack, rows, preferred_element_type=F32).astype(BF)

    def query_send(half):
        cols = pl.ds(0, 640) if half == 0 else pl.ds(640, 512)
        for i, (pz, pc) in enumerate(peers):
            sends.append(pltpu.make_async_remote_copy(
                src_ref=qs.at[pl.ds((pz * 2 + pc) * PACK, PACK), cols],
                dst_ref=qin.at[pl.ds(line * PACK, PACK), cols],
                send_sem=qs_sem.at[half, i], recv_sem=qr_sem.at[half],
                device_id=device(x, y, pz, pc), device_id_type=MESH))
            sends[-1].start()
        pltpu.make_async_copy(
            qs.at[pl.ds(line * PACK, PACK), cols], qin.at[pl.ds(line * PACK, PACK), cols],
            qr_sem.at[half]).start()

    pltpu.make_async_copy(zin, zin, zr_sem.at[0]).wait()
    aout[...] = jnp.dot(perm[...], zin[...], preferred_element_type=F32).astype(BF)
    for i, (px, py, pc) in enumerate(flat):
        sends.append(pltpu.make_async_remote_copy(
            src_ref=aout.at[pl.ds(block_id(px, py, pc) * 16, 16), :],
            dst_ref=ain.at[pl.ds(mine * 16, 16), :],
            send_sem=as_sem.at[i], recv_sem=ar_sem.at[0],
            device_id=device(px, py, z, pc), device_id_type=MESH))
        sends[-1].start()
    pltpu.make_async_copy(
        aout.at[pl.ds(mine * 16, 16), :], ain.at[pl.ds(mine * 16, 16), :], ar_sem.at[0]).start()

    query_block(0)

    pltpu.make_async_copy(ain, ain, ar_sem.at[0]).wait()
    got = ain[:, 2 * HS:].astype(F32)
    want = (lax.broadcasted_iota(jnp.int32, (512, HS), 1) + 1).astype(F32)
    one = jnp.concatenate([
        (got == want).astype(F32), (got == want + 128.0).astype(F32)], axis=1).astype(BF)
    kblk[...] = dot_t(one, ain[:, 0:HS]).astype(BF)
    vblk[...] = dot_t(ain[:, HS:2 * HS], one).astype(BF)

    def at_offset(a, b):
        return (x + a * (1 - c) + b * c) % 4, (y + a * c + b * (1 - c)) % 4

    def piece(q, a, b):
        px, py = at_offset(a, b)
        return (kall if q == 0 else vtall).at[block_id(px, py, c)]

    def source_of(q, a, b):
        if (a, b) == (0, 0):
            return kblk if q == 0 else vblk
        return piece(q, a, b)

    count = [0]

    def push(q, a, b, da, db):
        px, py = at_offset(da, db)
        sends.append(pltpu.make_async_remote_copy(
            src_ref=source_of(q, a, b), dst_ref=piece(q, a, b),
            send_sem=ts_sem.at[count[0]], recv_sem=tr_sem.at[q * 16 + (a - da) % 4 * 4 + (b - db) % 4],
            device_id=device(px, py, z, c), device_id_type=MESH))
        sends[-1].start()
        count[0] += 1

    def share(q, a, b):
        sends.append(pltpu.make_async_remote_copy(
            src_ref=source_of(q, a, b), dst_ref=piece(q, a, b),
            send_sem=ds_sem.at[q * 16 + a * 4 + b], recv_sem=dr_sem.at[q],
            device_id=device(x, y, z, 1 - c), device_id_type=MESH))
        sends[-1].start()

    local = [
        pltpu.make_async_copy(source_of(q, 0, 0), piece(q, 0, 0), loc_sem.at[q]) for q in range(2)]
    for da in (1, 3, 2):
        for q in range(2):
            push(q, 0, 0, da, 0)
    for db in (1, 3):
        for q in range(2):
            push(q, 0, 0, 0, db)
    for q in range(2):
        local[q].start()
        share(q, 0, 0)

    def arrive(q, a, b):
        ref = piece(q, a, b)
        pltpu.make_async_copy(ref, ref, tr_sem.at[q * 16 + a * 4 + b]).wait()
        if b == 0:
            push(q, a, b, 0, 1)
            push(q, a, b, 0, 3)
        elif b == (3, 1)[q]:
            push(q, a, b, 0, (1, 3)[q])
        share(q, a, b)

    query_block(1)
    query_send(0)
    for a, b in ((1, 0), (3, 0), (2, 0)):
        for q in range(2):
            arrive(q, a, b)
    query_block(2)
    for a, b in ((0, 1), (0, 3)):
        for q in range(2):
            arrive(q, a, b)
    query_block(3)
    query_send(1)
    for a, b in ((1, 1), (1, 3), (3, 1), (3, 3)):
        for q in range(2):
            arrive(q, a, b)

    pltpu.make_async_copy(qin.at[:, pl.ds(0, 640)], qin.at[:, pl.ds(0, 640)], qr_sem.at[0]).wait()
    shape = (NPACK, HS)
    i = lax.broadcasted_iota(jnp.int32, shape, 0)
    w = i - ((i * 43691) >> 21) * PACK
    base = ((w * 43691) >> 17) * 2 + c
    m = qin[:, 0:HS].astype(F32)
    slot = jnp.where(m > 0.0, base.astype(F32) * 256.0 + m - 1.0, 8192.0 + i.astype(F32))
    slot_row = jnp.transpose(slot)[0:1, :]
    slot_wide = jnp.concatenate([slot] * 3, axis=1)
    rank = jnp.sum((slot_row < slot_wide).astype(F32), axis=1, keepdims=True)
    lane = lax.broadcasted_iota(jnp.int32, (NPACK, NPACK), 1).astype(F32)
    one_o[...] = (lane == rank).astype(F32).astype(BF)

    for a, b in ((2, 1), (2, 3)):
        for q in range(2):
            arrive(q, a, b)

    rank_wide = jnp.broadcast_to(rank, shape)
    lane_q = (lax.broadcasted_iota(jnp.int32, shape, 1) & (CHUNK - 1)).astype(F32)
    lanes_o[...] = jnp.full_like(lanes_o, 8192)
    for n in range(NCHUNK):
        pick = rank_wide == lane_q + float(n * CHUNK)
        lanes_o[n:n + 1, :] = jnp.sum(
            jnp.where(pick, slot, 0.0), axis=0, keepdims=True).astype(jnp.int32)
    slots = lanes_o[...]
    start = starts(slots, ends)
    for n, v in enumerate((
        jnp.min(start, axis=1, keepdims=True),
        jnp.max(jnp.where(slots < 8192, slots, -1), axis=1, keepdims=True),
        jnp.max(start, axis=1, keepdims=True),
        jnp.min(slots, axis=1, keepdims=True),
    )):
        bounds_o[n * 16:(n + 1) * 16, :] = jnp.broadcast_to(v, (16, HS))
    pltpu.make_async_copy(qin.at[:, pl.ds(640, 512)], qin.at[:, pl.ds(640, 512)], qr_sem.at[1]).wait()
    qsort[...] = dot_t(one_o[...], qin[:, HS:]).astype(BF)

    for a, b in ((0, 2), (1, 2), (3, 2), (2, 2)):
        for q in range(2):
            arrive(q, a, b)
    other = pl.ds((1 - c) * 16, 16)
    pltpu.make_async_copy(kall.at[other], kall.at[other], dr_sem.at[0]).wait()
    pltpu.make_async_copy(vtall.at[other], vtall.at[other], dr_sem.at[1]).wait()
    for copy in local:
        copy.wait()
    for copy in sends:
        copy.wait_send()


def front(ends, tokens, wq, wk, wv, cos, sin, meta, pidx):
    anyspace = pl.BlockSpec(memory_space=pl.ANY)
    vmem = pl.BlockSpec(memory_space=pltpu.VMEM)
    dma = pltpu.SemaphoreType.DMA
    return pl.pallas_call(
        front_kernel,
        out_shape=(
            jax.ShapeDtypeStruct((NBLOCKS, ROWS, HS), BF),
            jax.ShapeDtypeStruct((NBLOCKS, HS, ROWS), BF),
            jax.ShapeDtypeStruct((NPACK, HQ * HS), BF),
            jax.ShapeDtypeStruct((NPACK, NPACK), BF),
            jax.ShapeDtypeStruct((16, HS), jnp.int32),
            jax.ShapeDtypeStruct((64, HS), jnp.int32),
        ),
        in_specs=[pl.BlockSpec(memory_space=pltpu.SMEM)] + [anyspace] * 4 + [vmem] * 4,
        out_specs=(anyspace, anyspace, vmem, vmem, vmem, vmem),
        scratch_shapes=[
            pltpu.VMEM((ROWS, D), BF),
            pltpu.VMEM((D, 2 * HS), BF),
            pltpu.VMEM((4, D, 256), BF),
            pltpu.VMEM((ROWS, 256), F32),
            pltpu.VMEM((NPACK, 3 * HS), BF),
            pltpu.VMEM((NPACK, 3 * HS), BF),
            pltpu.VMEM((512, NPACK), BF),
            pltpu.VMEM((512, 3 * HS), BF),
            pltpu.VMEM((512, 3 * HS), BF),
            pltpu.VMEM((ROWS, HS), BF),
            pltpu.VMEM((HS, ROWS), BF),
            pltpu.VMEM((NPACK, QW), BF),
            pltpu.VMEM((NPACK, QW), BF),
            dma((3, KPARTS)), dma((4,)), dma((3,)), dma((1,)), dma((31,)), dma((1,)),
            dma((2, 7)), dma((2,)), dma((30,)), dma((32,)), dma((32,)), dma((2,)), dma((2,)),
        ],
        compiler_params=pltpu.CompilerParams(
            collective_id=0, has_side_effects=True, vmem_limit_bytes=50 << 20),
        name="front",
    )(ends, tokens, wq, wk, wv, cos, sin, meta, pidx)


def attend_kernel(
    ends, bounds, lanes, qsort, one, kall, vtall, out, k_v, vt_v, osort, s_a, s_b, acc, load_sem,
):
    loads = []
    for g in range(4):
        part = pl.ds(g * 8, 8)
        loads.append((
            pltpu.make_async_copy(kall.at[part], k_v.at[part], load_sem.at[g]),
            pltpu.make_async_copy(vtall.at[part], vt_v.at[part], load_sem.at[4 + g]),
        ))
        for load in loads[g]:
            load.start()
    osort[...] = jnp.zeros_like(osort)
    scale = math.log2(math.e) / math.sqrt(HS)
    wide = CHUNK * HQ

    def chunk(n, ready):
        low, high, start_max, slot_min = (bounds[16 * v + n, 0] for v in range(4))

        need = high // (8 * ROWS) + 1
        for g in range(4):
            @pl.when((g >= ready) & (g < need))
            def _():
                for load in loads[g]:
                    load.wait()

        @pl.when(high >= 0)
        def _():
            rows = pl.ds(pl.multiple_of(n * CHUNK, CHUNK), CHUNK)
            queries = jnp.concatenate(
                [qsort[rows, h * HS:(h + 1) * HS] for h in range(HQ)], axis=0)
            half = lanes[pl.ds(n, 1), :]
            mine = jnp.concatenate([half, half], axis=1)
            begin = starts(mine, ends)

            def scores(t, ref):
                keys = k_v[t]
                ref[...] = lax.dot_general(
                    keys, queries, (((1,), (1,)), ((), ())), preferred_element_type=F32)

            first = low // KT
            last = high // KT + 1
            full_from = jnp.clip((start_max + KT - 1) // KT, first, last)
            full_to = jnp.clip((slot_min + 1) // KT, full_from, last)
            scores(2 * first, s_a)
            scores(2 * first + 1, s_b)
            acc[...] = jnp.zeros_like(acc)

            def tile(masked, t, state):
                top, total = state
                a = s_a[...]
                b = s_b[...]
                if masked:
                    at = lax.broadcasted_iota(jnp.int32, (ROWS, wide), 0)
                    begin_a, mine_a = begin - t * KT, mine - t * KT
                    begin_b, mine_b = begin_a - ROWS, mine_a - ROWS
                    a = jnp.where((at >= begin_a) & (at <= mine_a), a, -1e30)
                    b = jnp.where((at >= begin_b) & (at <= mine_b), b, -1e30)
                new = jnp.maximum(
                    top, jnp.max(jnp.maximum(a, b), axis=0, keepdims=True))
                shift = new * scale
                pa = jnp.exp2(a * scale - shift)
                pb = jnp.exp2(b * scale - shift)
                factor = jnp.exp2(top * scale - shift)
                total = total * factor + jnp.sum(pa + pb, axis=0, keepdims=True)
                after = jnp.minimum(t + 1, NBLOCKS // 2 - 1)
                scores(2 * after, s_a)
                scores(2 * after + 1, s_b)
                acc[...] = acc[...] * factor + (
                    jnp.dot(vt_v[2 * t], pa.astype(BF), preferred_element_type=F32)
                    + jnp.dot(vt_v[2 * t + 1], pb.astype(BF), preferred_element_type=F32))
                return new, total

            state = (jnp.full((1, wide), -1e30, F32), jnp.zeros((1, wide), F32))
            state = lax.fori_loop(first, full_from, functools.partial(tile, True), state)
            state = lax.fori_loop(full_from, full_to, functools.partial(tile, False), state)
            top, total = lax.fori_loop(full_to, last, functools.partial(tile, True), state)
            o = jnp.transpose(acc[...] / total).astype(BF)
            for h in range(HQ):
                osort[rows, h * HS:(h + 1) * HS] = o[h * CHUNK:(h + 1) * CHUNK, :]

        return jnp.maximum(ready, need)

    ready = lax.fori_loop(0, NCHUNK, chunk, 0)
    for g in range(4):
        @pl.when(g >= ready)
        def _():
            for load in loads[g]:
                load.wait()
    out[...] = jnp.dot(one[...], osort[...], preferred_element_type=F32).astype(BF)


def attend(ends, bounds, lanes, qsort, one, kall, vtall):
    vmem = pl.BlockSpec(memory_space=pltpu.VMEM)
    smem = pl.BlockSpec(memory_space=pltpu.SMEM)
    anyspace = pl.BlockSpec(memory_space=pl.ANY)
    wide = CHUNK * HQ
    return pl.pallas_call(
        attend_kernel,
        out_shape=jax.ShapeDtypeStruct((NPACK, HQ * HS), BF),
        in_specs=[smem, smem, vmem, vmem, vmem, anyspace, anyspace],
        out_specs=vmem,
        scratch_shapes=[
            pltpu.VMEM((NBLOCKS, ROWS, HS), BF),
            pltpu.VMEM((NBLOCKS, HS, ROWS), BF),
            pltpu.VMEM((NPACK, HQ * HS), BF),
            pltpu.VMEM((ROWS, wide), F32),
            pltpu.VMEM((ROWS, wide), F32),
            pltpu.VMEM((HS, wide), F32),
            pltpu.SemaphoreType.DMA((8,)),
        ],
        compiler_params=pltpu.CompilerParams(vmem_limit_bytes=40 << 20),
        name="attend",
    )(ends, bounds, lanes, qsort, one, kall, vtall)


def back_kernel(pidx, packed, out, ret, send_sem, recv_sem):
    x, y, z, c = place()
    line = z * 2 + c
    peers = []
    for dz in range(4):
        for dc in range(2):
            if (dz, dc) != (0, 0):
                peers.append(((z + dz) % 4, (c + dc) % 2))
    barrier = pltpu.get_barrier_semaphore()
    for pz, pc in peers:
        pl.semaphore_signal(barrier, inc=1, device_id=device(x, y, pz, pc), device_id_type=MESH)
    pl.semaphore_wait(barrier, 7)
    sends = []
    for i, (pz, pc) in enumerate(peers):
        sends.append(pltpu.make_async_remote_copy(
            src_ref=packed.at[pl.ds((pz * 2 + pc) * PACK, PACK), :],
            dst_ref=ret.at[pl.ds(line * PACK, PACK), :],
            send_sem=send_sem.at[i], recv_sem=recv_sem.at[0],
            device_id=device(x, y, pz, pc), device_id_type=MESH))
        sends[-1].start()
    pltpu.make_async_copy(
        packed.at[pl.ds(line * PACK, PACK), :], ret.at[pl.ds(line * PACK, PACK), :], recv_sem.at[0]).start()
    row = lax.broadcasted_iota(jnp.int32, (NPACK, ROWS), 0)
    pack = (row == pidx[...]).astype(F32).astype(BF)
    pltpu.make_async_copy(ret, ret, recv_sem.at[0]).wait()
    out[...] = dot_t(pack, ret[...]).astype(BF)
    for copy in sends:
        copy.wait_send()


def back(pidx, packed):
    anyspace = pl.BlockSpec(memory_space=pl.ANY)
    vmem = pl.BlockSpec(memory_space=pltpu.VMEM)
    return pl.pallas_call(
        back_kernel,
        out_shape=jax.ShapeDtypeStruct((ROWS, HQ * HS), BF),
        in_specs=[vmem, anyspace],
        out_specs=vmem,
        scratch_shapes=[pltpu.VMEM((NPACK, HQ * HS), BF), pltpu.SemaphoreType.DMA((7,)), pltpu.SemaphoreType.DMA((1,))],
        compiler_params=pltpu.CompilerParams(collective_id=1, has_side_effects=True),
        name="back",
    )(pidx, packed)


def shards(tokens, query_weight, key_weight, value_weight, doc_lengths, slot_index):
    x, y, z, c = place()
    order = jnp.arange(ROWS, dtype=jnp.int32)
    block = slot_index // ROWS
    same = block[:, None] == block[None, :]
    rank = jnp.sum((same & (order[None, :] < order[:, None])).astype(jnp.int32), axis=1)
    group = block // NBLOCKS
    local_block = block % NBLOCKS
    pidx = group * 96 + (local_block % 2) * PACK + (local_block // 2) * CAP + rank
    local = slot_index % (NBLOCKS * ROWS)
    ends = jnp.sum(jnp.where(
        jnp.arange(4)[None, :, None] >= jnp.arange(4)[None, None, :], doc_lengths[:, None, :], 0), axis=2)
    in_group = group[:, None] == jnp.arange(4, dtype=jnp.int32)[None, :]
    start = jnp.zeros_like(local)
    for d in range(3):
        end = jnp.sum(jnp.where(in_group, ends[:, d][None, :], 0), axis=1)
        start = jnp.where(local >= end, end, start)
    position = local - start
    frequency = 500000.0 ** (-(jnp.arange(HS // 2, dtype=F32) * 2.0 / HS))
    angles = position.astype(F32)[:, None] * frequency[None, :]
    cosine = jnp.cos(angles)
    sine = jnp.sin(angles)
    cos = jnp.concatenate([cosine, cosine], axis=1)
    sin = jnp.concatenate([-sine, sine], axis=1)
    meta = jnp.broadcast_to((slot_index % ROWS + 1).astype(BF)[:, None], (ROWS, HS))
    mine = jnp.sum(jnp.where(jnp.arange(4)[:, None] == z, ends, 0), axis=0)
    kall, vtall, qsort, one, lanes, bounds = front(
        mine, tokens, query_weight, key_weight, value_weight, cos, sin, meta, pidx[None, :])
    packed = attend(mine, bounds, lanes, qsort, one, kall, vtall)
    return back(pidx[None, :], packed)


def solution(mesh):
    in_specs = (P(("seq", "blk"), None), P(), P(), P(), P(), P(("seq", "blk")))
    out_specs = P(("seq", "blk"), None)
    return jax.shard_map(shards, mesh=mesh, in_specs=in_specs, out_specs=out_specs, check_vma=False)
```

```python
import functools
import math

import jax
import jax.numpy as jnp
from jax import lax
from jax.experimental import pallas as pl
from jax.experimental.pallas import tpu as pltpu
from jax.sharding import PartitionSpec as P

HQ = 8
HS = 128
D = 8192
ROWS = 256
NBLOCKS = 32
CAP = 3
PACK = 48
NPACK = 8 * PACK
QW = 128 + HQ * HS
KT = 512
KPARTS = 8
CHUNK = 32
NCHUNK = NPACK // CHUNK
MESH = pl.DeviceIdType.MESH
BF = jnp.bfloat16
F32 = jnp.float32
HIGHEST = lax.Precision.HIGHEST


def place():
    seq = lax.axis_index("seq")
    blk = lax.axis_index("blk")
    core = seq % 2
    y = (blk // 4) % 2 * 2 + seq // 2
    return blk // 8, y, blk % 4, core


def device(x, y, z, c):
    return ((y % 2) * 2 + c, (x * 2 + y // 2) * 4 + z)


def block_id(x, y, c):
    return c * 16 + x * 4 + y


def dot_t(a, b):
    return lax.dot_general(a, b, (((0,), (0,)), ((), ())), preferred_element_type=F32)


def rope(v, cos, sin):
    return v * cos + pltpu.roll(v, HS // 2, 1) * sin


def front_kernel(
    lengths, slot_ref, freq, tok, wq, wk, wv,
    kall, vtall, qsort, one_o, lanes_o, bounds_o, pack_o,
    cos, sin, tok_v, wkv_v, wq_v, acc, kvs, zin, perm, aout, ain, kblk, vblk, qs, qin,
    tok_sem, wq_sem, zs_sem, zr_sem, as_sem, ar_sem, qs_sem, qr_sem,
    ts_sem, tr_sem, ds_sem, dr_sem, loc_sem,
):
    x, y, z, c = place()
    kc = D // KPARTS
    mine = block_id(x, y, c)
    line = z * 2 + c

    loads = []
    for i in range(KPARTS):
        part = pl.ds(i * kc, kc)
        loads.append([
            pltpu.make_async_copy(tok.at[:, part], tok_v.at[:, part], tok_sem.at[0, i]),
            pltpu.make_async_copy(wk.at[part, :], wkv_v.at[part, pl.ds(0, HS)], tok_sem.at[1, i]),
            pltpu.make_async_copy(wv.at[part, :], wkv_v.at[part, pl.ds(HS, HS)], tok_sem.at[2, i]),
        ])
        for load in loads[i]:
            load.start()
    qloads = []
    for n in range(4):
        cols = pl.ds(n * 256, 256)
        qloads.append(pltpu.make_async_copy(wq.at[:, cols], wq_v.at[n], wq_sem.at[n]))

    peers = []
    for dz in range(4):
        for dc in range(2):
            if (dz, dc) != (0, 0):
                peers.append(((z + dz) % 4, (c + dc) % 2))
    flat = []
    for dx in range(4):
        for dy in range(4):
            for dc in range(2):
                if (dx, dy, dc) != (0, 0, 0):
                    flat.append(((x + dx) % 4, (y + dy) % 4, (c + dc) % 2))
    barrier = pltpu.get_barrier_semaphore()
    for pz, pc in peers:
        pl.semaphore_signal(barrier, inc=1, device_id=device(x, y, pz, pc), device_id_type=MESH)
    for px, py, pc in flat:
        pl.semaphore_signal(barrier, inc=1, device_id=device(px, py, z, pc), device_id_type=MESH)

    slot_r = slot_ref[...]
    block_r = slot_r >> 8
    slot_c = jnp.transpose(jnp.broadcast_to(slot_r.astype(F32), (HS, ROWS))).astype(jnp.int32)
    block_c = slot_c >> 8
    block_w = jnp.concatenate([block_c, block_c], axis=1)
    earlier = lax.broadcasted_iota(jnp.int32, (ROWS, ROWS), 0) < lax.broadcasted_iota(jnp.int32, (ROWS, ROWS), 1)
    rank_r = jnp.sum(
        ((block_w == block_r) & earlier).astype(F32), axis=0, keepdims=True).astype(jnp.int32)
    pidx = (block_r >> 5) * 96 + (block_r & 1) * PACK + ((block_r & 31) >> 1) * CAP + rank_r
    lane = lax.broadcasted_iota(jnp.int32, (NPACK, ROWS), 0)
    pack = (lane == pidx).astype(F32).astype(BF)
    pack_o[...] = pack
    meta = ((slot_c & 255) + 1).astype(F32).astype(BF)
    slots = jnp.dot(pack, meta, preferred_element_type=F32).astype(BF)
    kvs[:, 2 * HS:] = slots
    qs[:, 0:128] = slots
    local_c = slot_c & 8191
    group_c = slot_c >> 13
    start_c = jnp.zeros_like(slot_c)
    for g in range(4):
        end = 0
        for d in range(3):
            end = end + lengths[g, d]
            start_c = jnp.where((group_c == g) & (local_c >= end), end, start_c)
    angle = (local_c - start_c).astype(F32) * freq[...]
    cos[...] = jnp.cos(angle)
    sine = jnp.sin(angle)
    sin[...] = jnp.where(lax.broadcasted_iota(jnp.int32, (ROWS, HS), 1) < HS // 2, -sine, sine)

    for i in range(KPARTS):
        part = pl.ds(i * kc, kc)
        for load in loads[i]:
            load.wait()
        product = jnp.dot(tok_v[:, part], wkv_v[part, :], preferred_element_type=F32)
        if i == 0:
            acc[...] = product
        else:
            acc[...] += product
    for load in qloads:
        load.start()
    k_rows = rope(acc[:, :HS], cos[...], sin[...]).astype(BF)
    v_rows = acc[:, HS:].astype(BF)
    kvs[:, 0:HS] = jnp.dot(pack, k_rows, preferred_element_type=F32).astype(BF)
    kvs[:, HS:2 * HS] = jnp.dot(pack, v_rows, preferred_element_type=F32).astype(BF)

    pl.semaphore_wait(barrier, 7 + 31)

    sends = []
    for dz in range(1, 4):
        pz = (z + dz) % 4
        sends.append(pltpu.make_async_remote_copy(
            src_ref=kvs.at[pl.ds(pz * 96, 96), :], dst_ref=zin.at[pl.ds(z * 96, 96), :],
            send_sem=zs_sem.at[dz - 1], recv_sem=zr_sem.at[0],
            device_id=device(x, y, pz, c), device_id_type=MESH))
        sends[-1].start()
    pltpu.make_async_copy(
        kvs.at[pl.ds(z * 96, 96), :], zin.at[pl.ds(z * 96, 96), :], zr_sem.at[0]).start()

    def query_send(part):
        cols = (pl.ds(0, 128), pl.ds(128, 512), pl.ds(640, 512))[part]
        for i, (pz, pc) in enumerate(peers):
            sends.append(pltpu.make_async_remote_copy(
                src_ref=qs.at[pl.ds((pz * 2 + pc) * PACK, PACK), cols],
                dst_ref=qin.at[pl.ds(line * PACK, PACK), cols],
                send_sem=qs_sem.at[part, i], recv_sem=qr_sem.at[part],
                device_id=device(x, y, pz, pc), device_id_type=MESH))
            sends[-1].start()
        pltpu.make_async_copy(
            qs.at[pl.ds(line * PACK, PACK), cols], qin.at[pl.ds(line * PACK, PACK), cols],
            qr_sem.at[part]).start()

    def query_wait(part):
        cols = (pl.ds(0, 128), pl.ds(128, 512), pl.ds(640, 512))[part]
        pltpu.make_async_copy(qin.at[:, cols], qin.at[:, cols], qr_sem.at[part]).wait()

    def flush():
        while sends:
            sends.pop(0).wait_send()

    query_send(0)

    row = lax.broadcasted_iota(jnp.int32, (512, NPACK), 0)
    col = lax.broadcasted_iota(jnp.int32, (512, NPACK), 1)
    j = row >> 4
    slot12 = row & 15
    zz = (slot12 >= 3).astype(jnp.int32) + (slot12 >= 6).astype(jnp.int32) + (slot12 >= 9).astype(jnp.int32)
    source = zz * 96 + (j & 1) * 48 + (j >> 1) * 3 + (slot12 - 3 * zz)
    perm[...] = ((source == col) & (slot12 < 12)).astype(F32).astype(BF)

    def query_block(n):
        qloads[n].wait()
        acc[...] = jnp.zeros_like(acc)

        @pl.loop(0, 4)
        def _(i):
            part = pl.ds(pl.multiple_of(i * (D // 4), D // 4), D // 4)
            acc[...] += jnp.dot(tok_v[:, part], wq_v[n, part, :], preferred_element_type=F32)

        for h in range(2):
            rows = rope(acc[:, h * HS:(h + 1) * HS], cos[...], sin[...]).astype(BF)
            at = 128 + (n * 2 + h) * HS
            qs[:, at:at + HS] = jnp.dot(pack, rows, preferred_element_type=F32).astype(BF)

    query_block(0)

    pltpu.make_async_copy(zin, zin, zr_sem.at[0]).wait()
    aout[...] = jnp.dot(perm[...], zin[...], preferred_element_type=F32).astype(BF)
    for i, (px, py, pc) in enumerate(flat):
        sends.append(pltpu.make_async_remote_copy(
            src_ref=aout.at[pl.ds(block_id(px, py, pc) * 16, 16), :],
            dst_ref=ain.at[pl.ds(mine * 16, 16), :],
            send_sem=as_sem.at[i], recv_sem=ar_sem.at[0],
            device_id=device(px, py, z, pc), device_id_type=MESH))
        sends[-1].start()
    pltpu.make_async_copy(
        aout.at[pl.ds(mine * 16, 16), :], ain.at[pl.ds(mine * 16, 16), :], ar_sem.at[0]).start()

    query_block(1)
    query_send(1)
    query_block(2)

    query_wait(0)
    shape = (NPACK, HS)
    i = lax.broadcasted_iota(jnp.int32, shape, 0)
    w = i - ((i * 43691) >> 21) * PACK
    base = ((w * 43691) >> 17) * 2 + c
    m = qin[:, 0:HS].astype(F32)
    slot = jnp.where(m > 0.0, base.astype(F32) * 256.0 + m - 1.0, 8192.0 + i.astype(F32))
    slot_row = jnp.transpose(slot)[0:1, :]
    slot_wide = jnp.concatenate([slot] * 3, axis=1)
    rank = jnp.sum((slot_row < slot_wide).astype(F32), axis=1, keepdims=True)
    lane = lax.broadcasted_iota(jnp.int32, (NPACK, NPACK), 1).astype(F32)
    one_o[...] = (lane == rank).astype(F32).astype(BF)
    rank_wide = jnp.broadcast_to(rank, shape)
    lane_q = (lax.broadcasted_iota(jnp.int32, shape, 1) & (CHUNK - 1)).astype(F32)
    lanes_o[0:16, :] = jnp.full((16, HS), 8192, jnp.int32)
    for n in range(NCHUNK):
        pick = rank_wide == lane_q + float(n * CHUNK)
        lanes_o[n:n + 1, :] = jnp.sum(
            jnp.where(pick, slot, 0.0), axis=0, keepdims=True).astype(jnp.int32)
    slots = lanes_o[0:16, :]
    start = jnp.zeros_like(slots)
    end = 0
    for d in range(3):
        end = end + lengths[z, d]
        start = jnp.where(slots >= end, end, start)
    lanes_o[16:32, :] = start
    for n, v in enumerate((
        jnp.min(start, axis=1, keepdims=True),
        jnp.max(jnp.where(slots < 8192, slots, -1), axis=1, keepdims=True),
        jnp.max(start, axis=1, keepdims=True),
        jnp.min(slots, axis=1, keepdims=True),
    )):
        bounds_o[n * 16:(n + 1) * 16, :] = jnp.broadcast_to(v, (16, HS))

    query_block(3)
    query_send(2)

    pltpu.make_async_copy(ain, ain, ar_sem.at[0]).wait()
    got = ain[:, 2 * HS:].astype(F32)
    want = (lax.broadcasted_iota(jnp.int32, (512, HS), 1) + 1).astype(F32)
    one = jnp.concatenate([
        (got == want).astype(F32), (got == want + 128.0).astype(F32)], axis=1).astype(BF)
    kblk[...] = dot_t(one, ain[:, 0:HS]).astype(BF)
    vblk[...] = dot_t(ain[:, HS:2 * HS], one).astype(BF)

    def at_offset(a, b):
        return (x + a * (1 - c) + b * c) % 4, (y + a * c + b * (1 - c)) % 4

    def piece(q, a, b):
        px, py = at_offset(a, b)
        return (kall if q == 0 else vtall).at[block_id(px, py, c)]

    def source_of(q, a, b):
        if (a, b) == (0, 0):
            return kblk if q == 0 else vblk
        return piece(q, a, b)

    count = [0]

    def push(q, a, b, da, db):
        px, py = at_offset(da, db)
        sends.append(pltpu.make_async_remote_copy(
            src_ref=source_of(q, a, b), dst_ref=piece(q, a, b),
            send_sem=ts_sem.at[count[0]], recv_sem=tr_sem.at[q * 16 + (a - da) % 4 * 4 + (b - db) % 4],
            device_id=device(px, py, z, c), device_id_type=MESH))
        sends[-1].start()
        count[0] += 1

    def share(q, a, b):
        sends.append(pltpu.make_async_remote_copy(
            src_ref=source_of(q, a, b), dst_ref=piece(q, a, b),
            send_sem=ds_sem.at[q * 16 + a * 4 + b], recv_sem=dr_sem.at[q],
            device_id=device(x, y, z, 1 - c), device_id_type=MESH))
        sends[-1].start()

    local = [
        pltpu.make_async_copy(source_of(q, 0, 0), piece(q, 0, 0), loc_sem.at[q]) for q in range(2)]
    for da in (1, 3, 2):
        for q in range(2):
            push(q, 0, 0, da, 0)
    for db in (1, 3):
        for q in range(2):
            push(q, 0, 0, 0, db)
    for q in range(2):
        local[q].start()
        share(q, 0, 0)

    def arrive(q, a, b):
        ref = piece(q, a, b)
        pltpu.make_async_copy(ref, ref, tr_sem.at[q * 16 + a * 4 + b]).wait()
        if b == 0:
            push(q, a, b, 0, 1)
            push(q, a, b, 0, 3)
        elif b == (3, 1)[q]:
            push(q, a, b, 0, (1, 3)[q])
        share(q, a, b)

    for a, b in ((1, 0), (3, 0), (0, 1), (0, 3), (2, 0), (1, 1), (1, 3), (3, 1), (3, 3), (2, 1), (2, 3)):
        for q in range(2):
            arrive(q, a, b)
    query_wait(1)
    query_wait(2)
    qsort[...] = dot_t(one_o[...], qin[:, HS:]).astype(BF)
    while len(sends) > 36:
        sends.pop(0).wait_send()
    for a, b in ((0, 2), (1, 2), (3, 2), (2, 2)):
        for q in range(2):
            arrive(q, a, b)
    other = pl.ds((1 - c) * 16, 16)
    pltpu.make_async_copy(kall.at[other], kall.at[other], dr_sem.at[0]).wait()
    pltpu.make_async_copy(vtall.at[other], vtall.at[other], dr_sem.at[1]).wait()
    for copy in local:
        copy.wait()
    flush()


def front(lengths, slot_row, freq, tokens, wq, wk, wv):
    anyspace = pl.BlockSpec(memory_space=pl.ANY)
    vmem = pl.BlockSpec(memory_space=pltpu.VMEM)
    dma = pltpu.SemaphoreType.DMA
    return pl.pallas_call(
        front_kernel,
        out_shape=(
            jax.ShapeDtypeStruct((NBLOCKS, ROWS, HS), BF),
            jax.ShapeDtypeStruct((NBLOCKS, HS, ROWS), BF),
            jax.ShapeDtypeStruct((NPACK, HQ * HS), BF),
            jax.ShapeDtypeStruct((NPACK, NPACK), BF),
            jax.ShapeDtypeStruct((32, HS), jnp.int32),
            jax.ShapeDtypeStruct((64, HS), jnp.int32),
            jax.ShapeDtypeStruct((NPACK, ROWS), BF),
        ),
        in_specs=[pl.BlockSpec(memory_space=pltpu.SMEM), vmem, vmem] + [anyspace] * 4,
        out_specs=(anyspace, anyspace, vmem, vmem, vmem, vmem, vmem),
        scratch_shapes=[
            pltpu.VMEM((ROWS, HS), F32),
            pltpu.VMEM((ROWS, HS), F32),
            pltpu.VMEM((ROWS, D), BF),
            pltpu.VMEM((D, 2 * HS), BF),
            pltpu.VMEM((4, D, 256), BF),
            pltpu.VMEM((ROWS, 256), F32),
            pltpu.VMEM((NPACK, 3 * HS), BF),
            pltpu.VMEM((NPACK, 3 * HS), BF),
            pltpu.VMEM((512, NPACK), BF),
            pltpu.VMEM((512, 3 * HS), BF),
            pltpu.VMEM((512, 3 * HS), BF),
            pltpu.VMEM((ROWS, HS), BF),
            pltpu.VMEM((HS, ROWS), BF),
            pltpu.VMEM((NPACK, QW), BF),
            pltpu.VMEM((NPACK, QW), BF),
            dma((3, KPARTS)), dma((4,)), dma((3,)), dma((1,)), dma((31,)), dma((1,)),
            dma((3, 7)), dma((3,)), dma((30,)), dma((32,)), dma((32,)), dma((2,)), dma((2,)),
        ],
        compiler_params=pltpu.CompilerParams(
            collective_id=0, has_side_effects=True, vmem_limit_bytes=47 << 20),
        name="front",
    )(lengths, slot_row, freq, tokens, wq, wk, wv)


def attend_kernel(
    bounds, lanes, qsort, one, k_v, vt_v, out, osort, s_a, s_b, acc,
):
    osort[...] = jnp.zeros_like(osort)
    scale = math.log2(math.e) / math.sqrt(HS)
    wide = CHUNK * HQ

    def chunk(n, carry):
        low, high, start_max, slot_min = (bounds[16 * v + n, 0] for v in range(4))

        @pl.when(high >= 0)
        def _():
            rows = pl.ds(pl.multiple_of(n * CHUNK, CHUNK), CHUNK)
            queries = jnp.concatenate(
                [qsort[rows, h * HS:(h + 1) * HS] for h in range(HQ)], axis=0)
            half = lanes[pl.ds(n, 1), :]
            mine = jnp.concatenate([half, half], axis=1)
            half = lanes[pl.ds(n + 16, 1), :]
            begin = jnp.concatenate([half, half], axis=1)

            def scores(t, ref):
                keys = k_v[t]
                ref[...] = lax.dot_general(
                    keys, queries, (((1,), (1,)), ((), ())), preferred_element_type=F32)

            first = low // KT
            last = high // KT + 1
            full_from = jnp.clip((start_max + KT - 1) // KT, first, last)
            full_to = jnp.clip((slot_min + 1) // KT, full_from, last)
            scores(2 * first, s_a)
            scores(2 * first + 1, s_b)
            acc[...] = jnp.zeros_like(acc)

            def tile(masked, t, state):
                top, total = state
                a = s_a[...]
                b = s_b[...]
                if masked:
                    at = lax.broadcasted_iota(jnp.int32, (ROWS, wide), 0)
                    begin_a, mine_a = begin - t * KT, mine - t * KT
                    begin_b, mine_b = begin_a - ROWS, mine_a - ROWS
                    a = jnp.where((at >= begin_a) & (at <= mine_a), a, -1e30)
                    b = jnp.where((at >= begin_b) & (at <= mine_b), b, -1e30)
                new = jnp.maximum(
                    top, jnp.max(jnp.maximum(a, b), axis=0, keepdims=True))
                shift = new * scale
                pa = jnp.exp2(a * scale - shift)
                pb = jnp.exp2(b * scale - shift)
                factor = jnp.exp2(top * scale - shift)
                total = total * factor + jnp.sum(pa + pb, axis=0, keepdims=True)
                after = jnp.minimum(t + 1, NBLOCKS // 2 - 1)
                scores(2 * after, s_a)
                scores(2 * after + 1, s_b)
                acc[...] = acc[...] * factor + (
                    jnp.dot(vt_v[2 * t], pa.astype(BF), preferred_element_type=F32)
                    + jnp.dot(vt_v[2 * t + 1], pb.astype(BF), preferred_element_type=F32))
                return new, total

            state = (jnp.full((1, wide), -1e30, F32), jnp.zeros((1, wide), F32))
            state = lax.fori_loop(first, full_from, functools.partial(tile, True), state)
            state = lax.fori_loop(full_from, full_to, functools.partial(tile, False), state)
            top, total = lax.fori_loop(full_to, last, functools.partial(tile, True), state)
            o = jnp.transpose(acc[...] / total).astype(BF)
            for h in range(HQ):
                osort[rows, h * HS:(h + 1) * HS] = o[h * CHUNK:(h + 1) * CHUNK, :]

        return carry

    lax.fori_loop(0, NCHUNK, chunk, 0)
    out[...] = jnp.dot(one[...], osort[...], preferred_element_type=F32).astype(BF)


def attend(bounds, lanes, qsort, one, kall, vtall):
    vmem = pl.BlockSpec(memory_space=pltpu.VMEM)
    smem = pl.BlockSpec(memory_space=pltpu.SMEM)
    wide = CHUNK * HQ
    return pl.pallas_call(
        attend_kernel,
        out_shape=jax.ShapeDtypeStruct((NPACK, HQ * HS), BF),
        in_specs=[smem, vmem, vmem, vmem, vmem, vmem],
        out_specs=vmem,
        scratch_shapes=[
            pltpu.VMEM((NPACK, HQ * HS), BF),
            pltpu.VMEM((ROWS, wide), F32),
            pltpu.VMEM((ROWS, wide), F32),
            pltpu.VMEM((HS, wide), F32),
        ],
        compiler_params=pltpu.CompilerParams(vmem_limit_bytes=16 << 20),
        name="attend",
    )(bounds, lanes, qsort, one, kall, vtall)


def back_kernel(packed, ret, send_sem, recv_sem):
    x, y, z, c = place()
    line = z * 2 + c
    peers = []
    for dz in range(4):
        for dc in range(2):
            if (dz, dc) != (0, 0):
                peers.append(((z + dz) % 4, (c + dc) % 2))
    barrier = pltpu.get_barrier_semaphore()
    for pz, pc in peers:
        pl.semaphore_signal(barrier, inc=1, device_id=device(x, y, pz, pc), device_id_type=MESH)
    pl.semaphore_wait(barrier, 7)
    sends = []
    for i, (pz, pc) in enumerate(peers):
        sends.append(pltpu.make_async_remote_copy(
            src_ref=packed.at[pl.ds((pz * 2 + pc) * PACK, PACK), :],
            dst_ref=ret.at[pl.ds(line * PACK, PACK), :],
            send_sem=send_sem.at[i], recv_sem=recv_sem.at[0],
            device_id=device(x, y, pz, pc), device_id_type=MESH))
        sends[-1].start()
    pltpu.make_async_copy(
        packed.at[pl.ds(line * PACK, PACK), :], ret.at[pl.ds(line * PACK, PACK), :], recv_sem.at[0]).start()
    pltpu.make_async_copy(ret, ret, recv_sem.at[0]).wait()
    for copy in sends:
        copy.wait_send()


def back(packed):
    vmem = pl.BlockSpec(memory_space=pltpu.VMEM)
    return pl.pallas_call(
        back_kernel,
        out_shape=jax.ShapeDtypeStruct((NPACK, HQ * HS), BF),
        in_specs=[vmem],
        out_specs=pl.BlockSpec(memory_space=pl.ANY),
        scratch_shapes=[pltpu.SemaphoreType.DMA((7,)), pltpu.SemaphoreType.DMA((1,))],
        compiler_params=pltpu.CompilerParams(collective_id=1, has_side_effects=True, vmem_limit_bytes=4 << 20),
        name="back",
    )(packed)


def finish_kernel(pack, ret, out):
    out[...] = dot_t(pack[...], ret[...]).astype(BF)


def finish(pack, ret):
    vmem = pl.BlockSpec(memory_space=pltpu.VMEM)
    return pl.pallas_call(
        finish_kernel,
        out_shape=jax.ShapeDtypeStruct((ROWS, HQ * HS), BF),
        in_specs=[vmem, vmem],
        out_specs=vmem,
        compiler_params=pltpu.CompilerParams(vmem_limit_bytes=8 << 20),
        name="finish",
    )(pack, ret)


def shards(tokens, query_weight, key_weight, value_weight, doc_lengths, slot_index):
    frequency = 500000.0 ** (-(jnp.arange(HS // 2, dtype=F32) * 2.0 / HS))
    frequency = jnp.concatenate([frequency, frequency])[None, :]
    kall, vtall, qsort, one, lanes, bounds, pack = front(
        doc_lengths, slot_index[None, :], frequency, tokens, query_weight, key_weight, value_weight)
    packed = attend(bounds, lanes, qsort, one, kall, vtall)
    return finish(pack, back(packed))


def solution(mesh):
    in_specs = (P(("seq", "blk"), None), P(), P(), P(), P(), P(("seq", "blk")))
    out_specs = P(("seq", "blk"), None)
    return jax.shard_map(shards, mesh=mesh, in_specs=in_specs, out_specs=out_specs, check_vma=False)
```

```python
import functools
import math

import jax
import jax.numpy as jnp
from jax import lax
from jax.experimental import pallas as pl
from jax.experimental.pallas import tpu as pltpu
from jax.sharding import PartitionSpec as P

HQ = 8
HS = 128
D = 8192
ROWS = 256
NBLOCKS = 32
CAP = 3
PACK = 48
NPACK = 8 * PACK
QW = 128 + HQ * HS
KT = 1024
KPARTS = 8
CHUNK = 32
NCHUNK = NPACK // CHUNK
MESH = pl.DeviceIdType.MESH
BF = jnp.bfloat16
F32 = jnp.float32
HIGHEST = lax.Precision.HIGHEST


def place():
    seq = lax.axis_index("seq")
    blk = lax.axis_index("blk")
    core = seq % 2
    y = (blk // 4) % 2 * 2 + seq // 2
    return blk // 8, y, blk % 4, core


def device(x, y, z, c):
    return ((y % 2) * 2 + c, (x * 2 + y // 2) * 4 + z)


def block_id(x, y, c):
    return c * 16 + x * 4 + y


def dot_t(a, b):
    return lax.dot_general(a, b, (((0,), (0,)), ((), ())), preferred_element_type=F32)


def rope(v, cos, sin):
    return v * cos + pltpu.roll(v, HS // 2, 1) * sin


def front_kernel(
    lengths_ref, slot_hbm, freq, tok, wq, wk, wv,
    kall, vtall, qsort, one_o, lanes_o, bounds_o, pack_o,
    lengths, slot_ref, cos, sin, tok_v, wkv_v, wq_v, acc, kvs, zin, perm, aout, ain, kblk, vblk, qs, qin,
    tok_sem, wq_sem, zs_sem, zr_sem, as_sem, ar_sem, qs_sem, qr_sem,
    ts_sem, tr_sem, ds_sem, dr_sem, loc_sem, small_sem,
):
    x, y, z, c = place()
    kc = D // KPARTS
    mine = block_id(x, y, c)
    line = z * 2 + c

    small = [
        pltpu.make_async_copy(lengths_ref, lengths, small_sem.at[0]),
        pltpu.make_async_copy(slot_hbm, slot_ref, small_sem.at[1]),
    ]
    for load in small:
        load.start()
    loads = []
    for i in range(KPARTS):
        part = pl.ds(i * kc, kc)
        loads.append([
            pltpu.make_async_copy(tok.at[:, part], tok_v.at[:, part], tok_sem.at[0, i]),
            pltpu.make_async_copy(wk.at[part, :], wkv_v.at[part, pl.ds(0, HS)], tok_sem.at[1, i]),
            pltpu.make_async_copy(wv.at[part, :], wkv_v.at[part, pl.ds(HS, HS)], tok_sem.at[2, i]),
        ])
        for load in loads[i]:
            load.start()
    qloads = []
    for n in range(4):
        cols = pl.ds(n * 256, 256)
        qloads.append(pltpu.make_async_copy(wq.at[:, cols], wq_v.at[n], wq_sem.at[n]))

    peers = []
    for dz in range(4):
        for dc in range(2):
            if (dz, dc) != (0, 0):
                peers.append(((z + dz) % 4, (c + dc) % 2))
    flat = []
    for dx in range(4):
        for dy in range(4):
            for dc in range(2):
                if (dx, dy, dc) != (0, 0, 0):
                    flat.append(((x + dx) % 4, (y + dy) % 4, (c + dc) % 2))
    barrier = pltpu.get_barrier_semaphore()
    for pz, pc in peers:
        pl.semaphore_signal(barrier, inc=1, device_id=device(x, y, pz, pc), device_id_type=MESH)
    for px, py, pc in flat:
        pl.semaphore_signal(barrier, inc=1, device_id=device(px, py, z, pc), device_id_type=MESH)

    for load in small:
        load.wait()
    slot_r = slot_ref[...]
    block_r = slot_r >> 8
    slot_c = jnp.transpose(jnp.broadcast_to(slot_r.astype(F32), (HS, ROWS))).astype(jnp.int32)
    block_c = slot_c >> 8
    block_w = jnp.concatenate([block_c, block_c], axis=1)
    earlier = lax.broadcasted_iota(jnp.int32, (ROWS, ROWS), 0) < lax.broadcasted_iota(jnp.int32, (ROWS, ROWS), 1)
    rank_r = jnp.sum(
        ((block_w == block_r) & earlier).astype(F32), axis=0, keepdims=True).astype(jnp.int32)
    pidx = (block_r >> 5) * 96 + (block_r & 1) * PACK + ((block_r & 31) >> 1) * CAP + rank_r
    lane = lax.broadcasted_iota(jnp.int32, (NPACK, ROWS), 0)
    pack = (lane == pidx).astype(F32).astype(BF)
    pack_o[...] = pack
    meta = ((slot_c & 255) + 1).astype(F32).astype(BF)
    slots = jnp.dot(pack, meta, preferred_element_type=F32).astype(BF)
    kvs[:, 2 * HS:] = slots
    qs[:, 0:128] = slots
    local_c = slot_c & 8191
    group_c = slot_c >> 13
    start_c = jnp.zeros_like(slot_c)
    for g in range(4):
        end = 0
        for d in range(3):
            end = end + lengths[g, d]
            start_c = jnp.where((group_c == g) & (local_c >= end), end, start_c)
    angle = (local_c - start_c).astype(F32) * freq[...]
    cos[...] = jnp.cos(angle)
    sine = jnp.sin(angle)
    sin[...] = jnp.where(lax.broadcasted_iota(jnp.int32, (ROWS, HS), 1) < HS // 2, -sine, sine)

    for i in range(KPARTS):
        part = pl.ds(i * kc, kc)
        for load in loads[i]:
            load.wait()
        product = jnp.dot(tok_v[:, part], wkv_v[part, :], preferred_element_type=F32)
        if i == 0:
            acc[...] = product
        else:
            acc[...] += product
    for load in qloads:
        load.start()
    k_rows = rope(acc[:, :HS], cos[...], sin[...]).astype(BF)
    v_rows = acc[:, HS:].astype(BF)
    kvs[:, 0:HS] = jnp.dot(pack, k_rows, preferred_element_type=F32).astype(BF)
    kvs[:, HS:2 * HS] = jnp.dot(pack, v_rows, preferred_element_type=F32).astype(BF)

    pl.semaphore_wait(barrier, 7 + 31)

    sends = []
    for dz in range(1, 4):
        pz = (z + dz) % 4
        sends.append(pltpu.make_async_remote_copy(
            src_ref=kvs.at[pl.ds(pz * 96, 96), :], dst_ref=zin.at[pl.ds(z * 96, 96), :],
            send_sem=zs_sem.at[dz - 1], recv_sem=zr_sem.at[0],
            device_id=device(x, y, pz, c), device_id_type=MESH))
        sends[-1].start()
    pltpu.make_async_copy(
        kvs.at[pl.ds(z * 96, 96), :], zin.at[pl.ds(z * 96, 96), :], zr_sem.at[0]).start()

    def query_send(part):
        cols = (pl.ds(0, 128), pl.ds(128, 512), pl.ds(640, 512))[part]
        for i, (pz, pc) in enumerate(peers):
            sends.append(pltpu.make_async_remote_copy(
                src_ref=qs.at[pl.ds((pz * 2 + pc) * PACK, PACK), cols],
                dst_ref=qin.at[pl.ds(line * PACK, PACK), cols],
                send_sem=qs_sem.at[part, i], recv_sem=qr_sem.at[part],
                device_id=device(x, y, pz, pc), device_id_type=MESH))
            sends[-1].start()
        pltpu.make_async_copy(
            qs.at[pl.ds(line * PACK, PACK), cols], qin.at[pl.ds(line * PACK, PACK), cols],
            qr_sem.at[part]).start()

    def query_wait(part):
        cols = (pl.ds(0, 128), pl.ds(128, 512), pl.ds(640, 512))[part]
        pltpu.make_async_copy(qin.at[:, cols], qin.at[:, cols], qr_sem.at[part]).wait()

    def flush():
        while sends:
            sends.pop(0).wait_send()

    query_send(0)

    row = lax.broadcasted_iota(jnp.int32, (512, NPACK), 0)
    col = lax.broadcasted_iota(jnp.int32, (512, NPACK), 1)
    j = row >> 4
    slot12 = row & 15
    zz = (slot12 >= 3).astype(jnp.int32) + (slot12 >= 6).astype(jnp.int32) + (slot12 >= 9).astype(jnp.int32)
    source = zz * 96 + (j & 1) * 48 + (j >> 1) * 3 + (slot12 - 3 * zz)
    perm[...] = ((source == col) & (slot12 < 12)).astype(F32).astype(BF)

    def query_block(n):
        qloads[n].wait()
        acc[...] = jnp.zeros_like(acc)

        @pl.loop(0, 4)
        def _(i):
            part = pl.ds(pl.multiple_of(i * (D // 4), D // 4), D // 4)
            acc[...] += jnp.dot(tok_v[:, part], wq_v[n, part, :], preferred_element_type=F32)

        for h in range(2):
            rows = rope(acc[:, h * HS:(h + 1) * HS], cos[...], sin[...]).astype(BF)
            at = 128 + (n * 2 + h) * HS
            qs[:, at:at + HS] = jnp.dot(pack, rows, preferred_element_type=F32).astype(BF)

    query_block(0)

    pltpu.make_async_copy(zin, zin, zr_sem.at[0]).wait()
    aout[...] = jnp.dot(perm[...], zin[...], preferred_element_type=F32).astype(BF)
    for i, (px, py, pc) in enumerate(flat):
        sends.append(pltpu.make_async_remote_copy(
            src_ref=aout.at[pl.ds(block_id(px, py, pc) * 16, 16), :],
            dst_ref=ain.at[pl.ds(mine * 16, 16), :],
            send_sem=as_sem.at[i], recv_sem=ar_sem.at[0],
            device_id=device(px, py, z, pc), device_id_type=MESH))
        sends[-1].start()
    pltpu.make_async_copy(
        aout.at[pl.ds(mine * 16, 16), :], ain.at[pl.ds(mine * 16, 16), :], ar_sem.at[0]).start()

    query_block(1)
    query_send(1)
    query_block(2)

    query_wait(0)
    shape = (NPACK, HS)
    i = lax.broadcasted_iota(jnp.int32, shape, 0)
    w = i - ((i * 43691) >> 21) * PACK
    base = ((w * 43691) >> 17) * 2 + c
    m = qin[:, 0:HS].astype(F32)
    slot = jnp.where(m > 0.0, base.astype(F32) * 256.0 + m - 1.0, -1.0 - i.astype(F32))
    slot_row = jnp.transpose(slot)[0:1, :]
    slot_wide = jnp.concatenate([slot] * 3, axis=1)
    rank = jnp.sum((slot_row < slot_wide).astype(F32), axis=1, keepdims=True)
    lane = lax.broadcasted_iota(jnp.int32, (NPACK, NPACK), 1).astype(F32)
    one_o[...] = (lane == rank).astype(F32).astype(BF)
    rank_wide = jnp.broadcast_to(rank, shape)
    lane_q = (lax.broadcasted_iota(jnp.int32, shape, 1) & (CHUNK - 1)).astype(F32)
    lanes_o[0:16, :] = jnp.full((16, HS), -1, jnp.int32)
    for n in range(NCHUNK):
        pick = rank_wide == lane_q + float(n * CHUNK)
        lanes_o[n:n + 1, :] = jnp.sum(
            jnp.where(pick, slot, 0.0), axis=0, keepdims=True).astype(jnp.int32)
    slots = lanes_o[0:16, :]
    start = jnp.zeros_like(slots)
    end = 0
    for d in range(3):
        end = end + lengths[z, d]
        start = jnp.where(slots >= end, end, start)
    lanes_o[16:32, :] = start
    for n, v in enumerate((
        jnp.min(jnp.where(slots >= 0, start, 8192), axis=1, keepdims=True),
        jnp.max(slots, axis=1, keepdims=True),
        jnp.max(jnp.where(slots >= 0, start, 0), axis=1, keepdims=True),
        jnp.min(jnp.where(slots >= 0, slots, 8192), axis=1, keepdims=True),
    )):
        bounds_o[n * 16:(n + 1) * 16, :] = jnp.broadcast_to(v, (16, HS))

    query_block(3)
    query_send(2)

    pltpu.make_async_copy(ain, ain, ar_sem.at[0]).wait()
    got = ain[:, 2 * HS:].astype(F32)
    want = (lax.broadcasted_iota(jnp.int32, (512, HS), 1) + 1).astype(F32)
    one = jnp.concatenate([
        (got == want).astype(F32), (got == want + 128.0).astype(F32)], axis=1).astype(BF)
    kblk[...] = dot_t(one, ain[:, 0:HS]).astype(BF)
    vblk[...] = dot_t(ain[:, HS:2 * HS], one).astype(BF)

    def at_offset(a, b):
        return (x + a * (1 - c) + b * c) % 4, (y + a * c + b * (1 - c)) % 4

    def piece(q, a, b):
        px, py = at_offset(a, b)
        return (kall if q == 0 else vtall).at[block_id(px, py, c)]

    def source_of(q, a, b):
        if (a, b) == (0, 0):
            return kblk if q == 0 else vblk
        return piece(q, a, b)

    count = [0]

    def push(q, a, b, da, db):
        px, py = at_offset(da, db)
        sends.append(pltpu.make_async_remote_copy(
            src_ref=source_of(q, a, b), dst_ref=piece(q, a, b),
            send_sem=ts_sem.at[count[0]], recv_sem=tr_sem.at[q * 16 + (a - da) % 4 * 4 + (b - db) % 4],
            device_id=device(px, py, z, c), device_id_type=MESH))
        sends[-1].start()
        count[0] += 1

    def share(q, a, b):
        sends.append(pltpu.make_async_remote_copy(
            src_ref=source_of(q, a, b), dst_ref=piece(q, a, b),
            send_sem=ds_sem.at[q * 16 + a * 4 + b], recv_sem=dr_sem.at[q],
            device_id=device(x, y, z, 1 - c), device_id_type=MESH))
        sends[-1].start()

    local = [
        pltpu.make_async_copy(source_of(q, 0, 0), piece(q, 0, 0), loc_sem.at[q]) for q in range(2)]
    for da in (1, 3, 2):
        for q in range(2):
            push(q, 0, 0, da, 0)
    for db in (1, 3):
        for q in range(2):
            push(q, 0, 0, 0, db)
    for q in range(2):
        local[q].start()
        share(q, 0, 0)

    def arrive(q, a, b):
        ref = piece(q, a, b)
        pltpu.make_async_copy(ref, ref, tr_sem.at[q * 16 + a * 4 + b]).wait()
        if b == 0:
            push(q, a, b, 0, 1)
            push(q, a, b, 0, 3)
        elif b == (3, 1)[q]:
            push(q, a, b, 0, (1, 3)[q])
        share(q, a, b)

    for a, b in ((1, 0), (3, 0), (0, 1), (0, 3), (2, 0), (1, 1), (1, 3), (3, 1), (3, 3), (2, 1), (2, 3)):
        for q in range(2):
            arrive(q, a, b)
    query_wait(1)
    query_wait(2)
    qsort[...] = dot_t(one_o[...], qin[:, HS:]).astype(BF)
    while len(sends) > 36:
        sends.pop(0).wait_send()
    for a, b in ((0, 2), (1, 2), (3, 2), (2, 2)):
        for q in range(2):
            arrive(q, a, b)
    other = pl.ds((1 - c) * 16, 16)
    pltpu.make_async_copy(kall.at[other], kall.at[other], dr_sem.at[0]).wait()
    pltpu.make_async_copy(vtall.at[other], vtall.at[other], dr_sem.at[1]).wait()
    for copy in local:
        copy.wait()
    flush()


def front(lengths, slot_row, freq, tokens, wq, wk, wv):
    anyspace = pl.BlockSpec(memory_space=pl.ANY)
    vmem = pl.BlockSpec(memory_space=pltpu.VMEM)
    dma = pltpu.SemaphoreType.DMA
    hbm = pl.BlockSpec(memory_space=pltpu.HBM)
    return pl.pallas_call(
        front_kernel,
        out_shape=(
            jax.ShapeDtypeStruct((NBLOCKS, ROWS, HS), BF),
            jax.ShapeDtypeStruct((NBLOCKS, HS, ROWS), BF),
            jax.ShapeDtypeStruct((NPACK, HQ * HS), BF),
            jax.ShapeDtypeStruct((NPACK, NPACK), BF),
            jax.ShapeDtypeStruct((32, HS), jnp.int32),
            jax.ShapeDtypeStruct((64, HS), jnp.int32),
            jax.ShapeDtypeStruct((NPACK, ROWS), BF),
        ),
        in_specs=[hbm, hbm, vmem] + [anyspace] * 4,
        out_specs=(anyspace, anyspace, vmem, vmem, vmem, vmem, vmem),
        scratch_shapes=[
            pltpu.SMEM((4, 4), jnp.int32),
            pltpu.VMEM((1, ROWS), jnp.int32),
            pltpu.VMEM((ROWS, HS), F32),
            pltpu.VMEM((ROWS, HS), F32),
            pltpu.VMEM((ROWS, D), BF),
            pltpu.VMEM((D, 2 * HS), BF),
            pltpu.VMEM((4, D, 256), BF),
            pltpu.VMEM((ROWS, 256), F32),
            pltpu.VMEM((NPACK, 3 * HS), BF),
            pltpu.VMEM((NPACK, 3 * HS), BF),
            pltpu.VMEM((512, NPACK), BF),
            pltpu.VMEM((512, 3 * HS), BF),
            pltpu.VMEM((512, 3 * HS), BF),
            pltpu.VMEM((ROWS, HS), BF),
            pltpu.VMEM((HS, ROWS), BF),
            pltpu.VMEM((NPACK, QW), BF),
            pltpu.VMEM((NPACK, QW), BF),
            dma((3, KPARTS)), dma((4,)), dma((3,)), dma((1,)), dma((31,)), dma((1,)),
            dma((3, 7)), dma((3,)), dma((30,)), dma((32,)), dma((32,)), dma((2,)), dma((2,)), dma((2,)),
        ],
        compiler_params=pltpu.CompilerParams(
            collective_id=0, has_side_effects=True, vmem_limit_bytes=47 << 20),
        name="front",
    )(lengths, slot_row, freq, tokens, wq, wk, wv)


def attend_kernel(
    bounds, lanes, qsort, one, k_v, vt_v, out, osort, s_a, acc,
):
    osort[...] = jnp.zeros_like(osort)
    scale = math.log2(math.e) / math.sqrt(HS)
    wide = CHUNK * HQ

    def chunk(n, carry):
        low, high, start_max, slot_min = (bounds[16 * v + n, 0] for v in range(4))

        @pl.when(high >= 0)
        def _():
            rows = pl.ds(pl.multiple_of(n * CHUNK, CHUNK), CHUNK)
            queries = jnp.concatenate(
                [qsort[rows, h * HS:(h + 1) * HS] for h in range(HQ)], axis=0)
            half = lanes[pl.ds(n, 1), :]
            mine = jnp.concatenate([half, half], axis=1)
            half = lanes[pl.ds(n + 16, 1), :]
            begin = jnp.concatenate([half, half], axis=1)

            count = (high // ROWS - low // ROWS + 4) // 4
            first = jnp.maximum(high // ROWS + 1 - 4 * count, 0)
            origin = first * ROWS
            full_from = jnp.clip((start_max - origin + KT - 1) // KT - 1, 0, count - 1)
            full_to = jnp.clip((slot_min + 1 - origin) // KT - 1, full_from, count - 1)
            acc[...] = jnp.zeros_like(acc)

            def scores(masked, t):
                keys = k_v[pl.ds(first + 4 * t, 4)].reshape(KT, HS)
                s = scale * lax.dot_general(
                    keys, queries, (((1,), (1,)), ((), ())), preferred_element_type=F32)
                if masked:
                    at = lax.broadcasted_iota(jnp.int32, (KT, wide), 0)
                    base = origin + t * KT
                    s = jnp.where((at >= begin - base) & (at <= mine - base), s, -1e30)
                return s, jnp.max(s, axis=0, keepdims=True)

            def weigh(t, state):
                top, total, peak = state
                new = jnp.maximum(top, peak)
                p = jnp.exp2(s_a[...] - new)
                factor = jnp.exp2(top - new)
                total = total * factor + jnp.sum(p, axis=0, keepdims=True)
                values = jnp.concatenate([vt_v[first + 4 * t + u] for u in range(4)], axis=1)
                acc[...] = acc[...] * factor + jnp.dot(
                    values, p.astype(BF), preferred_element_type=F32)
                return new, total

            def tile(masked, t, state):
                s, peak = scores(masked, t + 1)
                new, total = weigh(t, state)
                s_a[...] = s
                return new, total, peak

            s, peak = scores(True, 0)
            s_a[...] = s
            state = (jnp.full((1, wide), -1e30, F32), jnp.zeros((1, wide), F32), peak)
            state = lax.fori_loop(0, full_from, functools.partial(tile, True), state)
            state = lax.fori_loop(full_from, full_to, functools.partial(tile, False), state)
            state = lax.fori_loop(full_to, count - 1, functools.partial(tile, True), state)
            top, total = weigh(count - 1, state)
            o = jnp.transpose(acc[...] / total).astype(BF)
            for h in range(HQ):
                osort[rows, h * HS:(h + 1) * HS] = o[h * CHUNK:(h + 1) * CHUNK, :]

        return carry

    lax.fori_loop(0, NCHUNK, chunk, 0)
    out[...] = jnp.dot(one[...], osort[...], preferred_element_type=F32).astype(BF)


def attend(bounds, lanes, qsort, one, kall, vtall):
    vmem = pl.BlockSpec(memory_space=pltpu.VMEM)
    smem = pl.BlockSpec(memory_space=pltpu.SMEM)
    wide = CHUNK * HQ
    return pl.pallas_call(
        attend_kernel,
        out_shape=jax.ShapeDtypeStruct((NPACK, HQ * HS), BF),
        in_specs=[smem, vmem, vmem, vmem, vmem, vmem],
        out_specs=vmem,
        scratch_shapes=[
            pltpu.VMEM((NPACK, HQ * HS), BF),
            pltpu.VMEM((KT, wide), F32),
            pltpu.VMEM((HS, wide), F32),
        ],
        compiler_params=pltpu.CompilerParams(vmem_limit_bytes=16 << 20),
        name="attend",
    )(bounds, lanes, qsort, one, kall, vtall)


def back_kernel(packed, ret, send_sem, recv_sem):
    x, y, z, c = place()
    line = z * 2 + c
    peers = []
    for dz in range(4):
        for dc in range(2):
            if (dz, dc) != (0, 0):
                peers.append(((z + dz) % 4, (c + dc) % 2))
    barrier = pltpu.get_barrier_semaphore()
    for pz, pc in peers:
        pl.semaphore_signal(barrier, inc=1, device_id=device(x, y, pz, pc), device_id_type=MESH)
    pl.semaphore_wait(barrier, 7)
    sends = []
    for i, (pz, pc) in enumerate(peers):
        sends.append(pltpu.make_async_remote_copy(
            src_ref=packed.at[pl.ds((pz * 2 + pc) * PACK, PACK), :],
            dst_ref=ret.at[pl.ds(line * PACK, PACK), :],
            send_sem=send_sem.at[i], recv_sem=recv_sem.at[0],
            device_id=device(x, y, pz, pc), device_id_type=MESH))
        sends[-1].start()
    pltpu.make_async_copy(
        packed.at[pl.ds(line * PACK, PACK), :], ret.at[pl.ds(line * PACK, PACK), :], recv_sem.at[0]).start()
    pltpu.make_async_copy(ret, ret, recv_sem.at[0]).wait()
    for copy in sends:
        copy.wait_send()


def back(packed):
    vmem = pl.BlockSpec(memory_space=pltpu.VMEM)
    return pl.pallas_call(
        back_kernel,
        out_shape=jax.ShapeDtypeStruct((NPACK, HQ * HS), BF),
        in_specs=[vmem],
        out_specs=pl.BlockSpec(memory_space=pl.ANY),
        scratch_shapes=[pltpu.SemaphoreType.DMA((7,)), pltpu.SemaphoreType.DMA((1,))],
        compiler_params=pltpu.CompilerParams(collective_id=1, has_side_effects=True, vmem_limit_bytes=4 << 20),
        name="back",
    )(packed)


def finish_kernel(pack, ret, out):
    out[...] = dot_t(pack[...], ret[...]).astype(BF)


def finish(pack, ret):
    vmem = pl.BlockSpec(memory_space=pltpu.VMEM)
    return pl.pallas_call(
        finish_kernel,
        out_shape=jax.ShapeDtypeStruct((ROWS, HQ * HS), BF),
        in_specs=[vmem, vmem],
        out_specs=vmem,
        compiler_params=pltpu.CompilerParams(vmem_limit_bytes=8 << 20),
        name="finish",
    )(pack, ret)


def shards(tokens, query_weight, key_weight, value_weight, doc_lengths, slot_index):
    frequency = 500000.0 ** (-(jnp.arange(HS // 2, dtype=F32) * 2.0 / HS))
    frequency = jnp.concatenate([frequency, frequency])[None, :]
    kall, vtall, qsort, one, lanes, bounds, pack = front(
        doc_lengths, slot_index[None, :], frequency, tokens, query_weight, key_weight, value_weight)
    packed = attend(bounds, lanes, qsort, one, kall, vtall)
    return finish(pack, back(packed))


def solution(mesh):
    in_specs = (P(("seq", "blk"), None), P(), P(), P(), P(), P(("seq", "blk")))
    out_specs = P(("seq", "blk"), None)
    return jax.shard_map(shards, mesh=mesh, in_specs=in_specs, out_specs=out_specs, check_vma=False)
```

```python
import functools
import math

import jax
import jax.numpy as jnp
from jax import lax
from jax.experimental import pallas as pl
from jax.experimental.pallas import tpu as pltpu
from jax.sharding import PartitionSpec as P

HQ = 8
HS = 128
D = 8192
ROWS = 256
NBLOCKS = 32
CAP = 3
PACK = 48
NPACK = 8 * PACK
QW = 128 + HQ * HS
KT = 1024
KPARTS = 8
CHUNK = 32
NCHUNK = NPACK // CHUNK
MESH = pl.DeviceIdType.MESH
BF = jnp.bfloat16
F32 = jnp.float32
HIGHEST = lax.Precision.HIGHEST


def place():
    seq = lax.axis_index("seq")
    blk = lax.axis_index("blk")
    core = seq % 2
    y = (blk // 4) % 2 * 2 + seq // 2
    return blk // 8, y, blk % 4, core


def device(x, y, z, c):
    return ((y % 2) * 2 + c, (x * 2 + y // 2) * 4 + z)


def block_id(x, y, c):
    return c * 16 + x * 4 + y


def dot_t(a, b):
    return lax.dot_general(a, b, (((0,), (0,)), ((), ())), preferred_element_type=F32)


def rope(v, cos, sin):
    return v * cos + pltpu.roll(v, HS // 2, 1) * sin


def front_kernel(
    ints, freq, tok, wq, wk, wv,
    kall, vtall, qsort, one_o, lanes_o, bounds_o, pack_o,
    lengths, cos, sin, tok_v, wkv_v, wq_v, acc, kvs, zin, perm, aout, ain, kblk, vblk, qs, qin,
    tok_sem, wq_sem, zs_sem, zr_sem, as_sem, ar_sem, qs_sem, qr_sem,
    ts_sem, tr_sem, dr_sem, loc_sem, small_sem,
):
    x, y, z, c = place()
    xs, ys, zs = ([v if n == 0 else (v + n) % 4 for n in range(4)] for v in (x, y, z))
    low, high = [v % 2 * 2 for v in ys], [v // 2 * 4 for v in ys]
    cs = [c, 1 - c]
    kc = D // KPARTS
    mine = block_id(x, y, c)

    def at(dx, dy, dz, dc):
        return low[dy] + cs[dc], xs[dx] * 8 + high[dy] + zs[dz]

    line = z * 2 + c

    small = pltpu.make_async_copy(ints, lengths, small_sem.at[0])
    small.start()
    loads = []
    for i in range(KPARTS):
        part = pl.ds(i * kc, kc)
        loads.append([
            pltpu.make_async_copy(tok.at[:, part], tok_v.at[:, part], tok_sem.at[0, i]),
            pltpu.make_async_copy(wk.at[part, :], wkv_v.at[part, pl.ds(0, HS)], tok_sem.at[1, i]),
            pltpu.make_async_copy(wv.at[part, :], wkv_v.at[part, pl.ds(HS, HS)], tok_sem.at[2, i]),
        ])
        for load in loads[i]:
            load.start()
    qloads = []
    for n in range(4):
        cols = pl.ds(n * 256, 256)
        qloads.append(pltpu.make_async_copy(wq.at[:, cols], wq_v.at[n], wq_sem.at[n]))

    peers = [(dz, dc) for dz in range(4) for dc in range(2)][1:]
    flat = [(dx, dy, dc) for dx in range(4) for dy in range(4) for dc in range(2)][1:]
    barrier = pltpu.get_barrier_semaphore()
    for dz, dc in peers:
        pl.semaphore_signal(barrier, inc=1, device_id=at(0, 0, dz, dc), device_id_type=MESH)
    for dx, dy, dc in flat:
        pl.semaphore_signal(barrier, inc=1, device_id=at(dx, dy, 0, dc), device_id_type=MESH)

    slot_r = ints[0:1, :]
    block_r = slot_r >> 8
    slot_c = jnp.transpose(jnp.broadcast_to(slot_r.astype(F32), (HS, ROWS))).astype(jnp.int32)
    block_c = slot_c >> 8
    block_w = jnp.concatenate([block_c, block_c], axis=1)
    earlier = lax.broadcasted_iota(jnp.int32, (ROWS, ROWS), 0) < lax.broadcasted_iota(jnp.int32, (ROWS, ROWS), 1)
    rank_r = jnp.sum(
        ((block_w == block_r) & earlier).astype(F32), axis=0, keepdims=True).astype(jnp.int32)
    pidx = (block_r >> 5) * 96 + (block_r & 1) * PACK + ((block_r & 31) >> 1) * CAP + rank_r
    lane = lax.broadcasted_iota(jnp.int32, (NPACK, ROWS), 0)
    pack = (lane == pidx).astype(F32).astype(BF)
    pack_o[...] = pack
    meta = ((slot_c & 255) + 1).astype(F32).astype(BF)
    slots = jnp.dot(pack, meta, preferred_element_type=F32).astype(BF)
    kvs[:, 2 * HS:] = slots
    qs[:, 0:128] = slots
    small.wait()
    local_c = slot_c & 8191
    group_c = slot_c >> 13
    start_c = jnp.zeros_like(slot_c)
    for g in range(4):
        end = 0
        for d in range(3):
            end = end + lengths[1 + g, d]
            start_c = jnp.where((group_c == g) & (local_c >= end), end, start_c)
    angle = (local_c - start_c).astype(F32) * freq[...]
    left = lax.broadcasted_iota(jnp.int32, (HS, HS), 1) < HS // 2
    angle = jnp.where(left, angle[:HS], angle[HS:])
    cosine, sine = jnp.cos(angle), jnp.sin(angle)
    cosine_r, sine_r = pltpu.roll(cosine, HS // 2, 1), pltpu.roll(sine, HS // 2, 1)
    cos[0:HS, :] = jnp.where(left, cosine, cosine_r)
    cos[HS:, :] = jnp.where(left, cosine_r, cosine)
    sin[0:HS, :] = jnp.where(left, -sine, sine_r)
    sin[HS:, :] = jnp.where(left, -sine_r, sine)

    for i in range(KPARTS):
        part = pl.ds(i * kc, kc)
        for load in loads[i]:
            load.wait()
        product = jnp.dot(tok_v[:, part], wkv_v[part, :], preferred_element_type=F32)
        if i == 0:
            acc[...] = product
        else:
            acc[...] += product
    for load in qloads:
        load.start()
    k_rows = rope(acc[:, :HS], cos[...], sin[...]).astype(BF)
    v_rows = acc[:, HS:].astype(BF)
    kvs[:, 0:HS] = jnp.dot(pack, k_rows, preferred_element_type=F32).astype(BF)
    kvs[:, HS:2 * HS] = jnp.dot(pack, v_rows, preferred_element_type=F32).astype(BF)

    pl.semaphore_wait(barrier, 7 + 31)

    for dz in range(1, 4):
        pltpu.make_async_remote_copy(
            src_ref=kvs.at[pl.ds(zs[dz] * 96, 96), :], dst_ref=zin.at[pl.ds(z * 96, 96), :],
            send_sem=zs_sem.at[0], recv_sem=zr_sem.at[0],
            device_id=at(0, 0, dz, 0), device_id_type=MESH).start()
    pltpu.make_async_copy(
        kvs.at[pl.ds(z * 96, 96), :], zin.at[pl.ds(z * 96, 96), :], zr_sem.at[0]).start()

    columns = (pl.ds(0, 128), pl.ds(128, 512), pl.ds(640, 512))

    def query_send(part):
        cols = columns[part]
        for dz, dc in peers:
            pltpu.make_async_remote_copy(
                src_ref=qs.at[pl.ds((zs[dz] * 2 + cs[dc]) * PACK, PACK), cols],
                dst_ref=qin.at[pl.ds(line * PACK, PACK), cols],
                send_sem=qs_sem.at[part], recv_sem=qr_sem.at[part],
                device_id=at(0, 0, dz, dc), device_id_type=MESH).start()
        pltpu.make_async_copy(
            qs.at[pl.ds(line * PACK, PACK), cols], qin.at[pl.ds(line * PACK, PACK), cols],
            qr_sem.at[part]).start()

    def query_wait(part):
        cols = columns[part]
        pltpu.make_async_copy(qin.at[:, cols], qin.at[:, cols], qr_sem.at[part]).wait()

    def sent(ref, sem):
        pltpu.make_async_copy(ref, ref, sem).wait()

    query_send(0)

    row = lax.broadcasted_iota(jnp.int32, (512, NPACK), 0)
    col = lax.broadcasted_iota(jnp.int32, (512, NPACK), 1)
    j = row >> 4
    slot12 = row & 15
    zz = (slot12 >= 3).astype(jnp.int32) + (slot12 >= 6).astype(jnp.int32) + (slot12 >= 9).astype(jnp.int32)
    source = zz * 96 + (j & 1) * 48 + (j >> 1) * 3 + (slot12 - 3 * zz)
    perm[...] = ((source == col) & (slot12 < 12)).astype(F32).astype(BF)

    def query_block(n):
        qloads[n].wait()
        acc[...] = jnp.zeros_like(acc)

        @pl.loop(0, 4)
        def _(i):
            part = pl.ds(pl.multiple_of(i * (D // 4), D // 4), D // 4)
            acc[...] += jnp.dot(tok_v[:, part], wq_v[n, part, :], preferred_element_type=F32)

        for h in range(2):
            rows = rope(acc[:, h * HS:(h + 1) * HS], cos[...], sin[...]).astype(BF)
            at = 128 + (n * 2 + h) * HS
            qs[:, at:at + HS] = jnp.dot(pack, rows, preferred_element_type=F32).astype(BF)

    query_block(0)

    pltpu.make_async_copy(zin, zin, zr_sem.at[0]).wait()
    aout[...] = jnp.dot(perm[...], zin[...], preferred_element_type=F32).astype(BF)
    for dx, dy, dc in flat:
        pltpu.make_async_remote_copy(
            src_ref=aout.at[pl.ds(block_id(xs[dx], ys[dy], cs[dc]) * 16, 16), :],
            dst_ref=ain.at[pl.ds(mine * 16, 16), :],
            send_sem=as_sem.at[0], recv_sem=ar_sem.at[0],
            device_id=at(dx, dy, 0, dc), device_id_type=MESH).start()
    pltpu.make_async_copy(
        aout.at[pl.ds(mine * 16, 16), :], ain.at[pl.ds(mine * 16, 16), :], ar_sem.at[0]).start()

    query_block(1)
    query_send(1)
    query_block(2)

    query_wait(0)
    shape = (NPACK, HS)
    i = lax.broadcasted_iota(jnp.int32, shape, 0)
    w = i - ((i * 43691) >> 21) * PACK
    base = ((w * 43691) >> 17) * 2 + c
    m = qin[:, 0:HS].astype(F32)
    slot = jnp.where(m > 0.0, base.astype(F32) * 256.0 + m - 1.0, -1.0 - i.astype(F32))
    slot_row = jnp.transpose(slot)[0:1, :]
    slot_wide = jnp.concatenate([slot] * 3, axis=1)
    rank = jnp.sum((slot_row < slot_wide).astype(F32), axis=1, keepdims=True)
    lane = lax.broadcasted_iota(jnp.int32, (NPACK, NPACK), 1).astype(F32)
    one_o[...] = (lane == rank).astype(F32).astype(BF)
    rank_wide = jnp.broadcast_to(rank, shape)
    lane_q = (lax.broadcasted_iota(jnp.int32, shape, 1) & (CHUNK - 1)).astype(F32)
    lanes_o[0:16, :] = jnp.full((16, HS), -1, jnp.int32)
    for n in range(NCHUNK):
        pick = rank_wide == lane_q + float(n * CHUNK)
        lanes_o[n:n + 1, :] = jnp.sum(
            jnp.where(pick, slot, 0.0), axis=0, keepdims=True).astype(jnp.int32)
    slots = lanes_o[0:16, :]
    start = jnp.zeros_like(slots)
    end = 0
    for d in range(3):
        end = end + lengths[1 + z, d]
        start = jnp.where(slots >= end, end, start)
    lanes_o[16:32, :] = start
    for n, v in enumerate((
        jnp.min(jnp.where(slots >= 0, start, 8192), axis=1, keepdims=True),
        jnp.max(slots, axis=1, keepdims=True),
        jnp.max(jnp.where(slots >= 0, start, 0), axis=1, keepdims=True),
        jnp.min(jnp.where(slots >= 0, slots, 8192), axis=1, keepdims=True),
    )):
        bounds_o[n * 16:(n + 1) * 16, :] = jnp.broadcast_to(v, (16, HS))

    query_block(3)
    query_send(2)

    pltpu.make_async_copy(ain, ain, ar_sem.at[0]).wait()
    got = ain[:, 2 * HS:].astype(F32)
    want = (lax.broadcasted_iota(jnp.int32, (512, HS), 1) + 1).astype(F32)
    one = jnp.concatenate([
        (got == want).astype(F32), (got == want + 128.0).astype(F32)], axis=1).astype(BF)
    kblk[...] = dot_t(one, ain[:, 0:HS]).astype(BF)
    vblk[...] = dot_t(ain[:, HS:2 * HS], one).astype(BF)

    blocks = [[
        (xs[a] + (xs[b] - xs[a]) * c) * 4 + ys[b] + (ys[a] - ys[b]) * c + 16 * c
        for b in range(4)] for a in range(4)]

    def along(a, b):
        one, two = at(a, b, 0, 0), at(b, a, 0, 0)
        return tuple(u + (v - u) * c for u, v in zip(one, two))

    first, second = [None] + [along(n, 0) for n in (1, 2, 3)], [None] + [along(0, n) for n in (1, 2, 3)]

    def piece(q, a, b):
        return (kall if q == 0 else vtall).at[blocks[a][b]]

    def source_of(q, a, b):
        if (a, b) == (0, 0):
            return kblk if q == 0 else vblk
        return piece(q, a, b)

    def push(q, a, b, da, db):
        pltpu.make_async_remote_copy(
            src_ref=source_of(q, a, b), dst_ref=piece(q, a, b),
            send_sem=ts_sem.at[q], recv_sem=tr_sem.at[q * 16 + (a - da) % 4 * 4 + (b - db) % 4],
            device_id=first[da] if db == 0 else second[db], device_id_type=MESH).start()

    partner = at(0, 0, 0, 1)

    def share(q, a, b):
        pltpu.make_async_remote_copy(
            src_ref=source_of(q, a, b), dst_ref=piece(q, a, b),
            send_sem=ts_sem.at[q], recv_sem=dr_sem.at[q],
            device_id=partner, device_id_type=MESH).start()

    local = [
        pltpu.make_async_copy(source_of(q, 0, 0), piece(q, 0, 0), loc_sem.at[q]) for q in range(2)]
    for da in (1, 3, 2):
        for q in range(2):
            push(q, 0, 0, da, 0)
    for db in (1, 3):
        for q in range(2):
            push(q, 0, 0, 0, db)
    for q in range(2):
        local[q].start()
        share(q, 0, 0)

    def arrive(q, a, b):
        ref = piece(q, a, b)
        pltpu.make_async_copy(ref, ref, tr_sem.at[q * 16 + a * 4 + b]).wait()
        if b == 0:
            push(q, a, b, 0, 1)
            push(q, a, b, 0, 3)
        elif b == (3, 1)[q]:
            push(q, a, b, 0, (1, 3)[q])
        share(q, a, b)

    for a, b in ((1, 0), (3, 0), (0, 1), (0, 3), (2, 0), (1, 1), (1, 3), (3, 1), (3, 3), (2, 1), (2, 3)):
        for q in range(2):
            arrive(q, a, b)
    query_wait(1)
    query_wait(2)
    qsort[...] = dot_t(one_o[...], qin[:, HS:]).astype(BF)
    sent(zin.at[pl.ds(0, 288), :], zs_sem.at[0])
    sent(aout.at[pl.ds(0, 31 * 16), :], as_sem.at[0])
    for n, cols in enumerate(columns):
        sent(qs.at[pl.ds(0, 7 * PACK), cols], qs_sem.at[n])
    for a, b in ((0, 2), (1, 2), (3, 2), (2, 2)):
        for q in range(2):
            arrive(q, a, b)
    other = pl.ds((1 - c) * 16, 16)
    pltpu.make_async_copy(kall.at[other], kall.at[other], dr_sem.at[0]).wait()
    pltpu.make_async_copy(vtall.at[other], vtall.at[other], dr_sem.at[1]).wait()
    for copy in local:
        copy.wait()
    sent(kall.at[pl.ds(0, 31)], ts_sem.at[0])
    sent(vtall.at[pl.ds(0, 31)], ts_sem.at[1])


def front(ints, freq, tokens, wq, wk, wv):
    anyspace = pl.BlockSpec(memory_space=pl.ANY)
    vmem = pl.BlockSpec(memory_space=pltpu.VMEM)
    dma = pltpu.SemaphoreType.DMA
    return pl.pallas_call(
        front_kernel,
        out_shape=(
            jax.ShapeDtypeStruct((NBLOCKS, ROWS, HS), BF),
            jax.ShapeDtypeStruct((NBLOCKS, HS, ROWS), BF),
            jax.ShapeDtypeStruct((NPACK, HQ * HS), BF),
            jax.ShapeDtypeStruct((NPACK, NPACK), BF),
            jax.ShapeDtypeStruct((32, HS), jnp.int32),
            jax.ShapeDtypeStruct((64, HS), jnp.int32),
            jax.ShapeDtypeStruct((NPACK, ROWS), BF),
        ),
        in_specs=[vmem, vmem] + [anyspace] * 4,
        out_specs=(anyspace, anyspace, vmem, vmem, vmem, vmem, vmem),
        scratch_shapes=[
            pltpu.SMEM((8, ROWS), jnp.int32),
            pltpu.VMEM((ROWS, HS), F32),
            pltpu.VMEM((ROWS, HS), F32),
            pltpu.VMEM((ROWS, D), BF),
            pltpu.VMEM((D, 2 * HS), BF),
            pltpu.VMEM((4, D, 256), BF),
            pltpu.VMEM((ROWS, 256), F32),
            pltpu.VMEM((NPACK, 3 * HS), BF),
            pltpu.VMEM((NPACK, 3 * HS), BF),
            pltpu.VMEM((512, NPACK), BF),
            pltpu.VMEM((512, 3 * HS), BF),
            pltpu.VMEM((512, 3 * HS), BF),
            pltpu.VMEM((ROWS, HS), BF),
            pltpu.VMEM((HS, ROWS), BF),
            pltpu.VMEM((NPACK, QW), BF),
            pltpu.VMEM((NPACK, QW), BF),
            dma((3, KPARTS)), dma((4,)), dma((1,)), dma((1,)), dma((1,)), dma((1,)),
            dma((3,)), dma((3,)), dma((2,)), dma((32,)), dma((2,)), dma((2,)), dma((1,)),
        ],
        compiler_params=pltpu.CompilerParams(
            collective_id=0, has_side_effects=True, vmem_limit_bytes=47 << 20),
        name="front",
    )(ints, freq, tokens, wq, wk, wv)


def attend_kernel(
    bounds, lanes, qsort, one, k_v, vt_v, out, osort, s_a, acc,
):
    osort[...] = jnp.zeros_like(osort)
    scale = math.log2(math.e) / math.sqrt(HS)
    wide = CHUNK * HQ

    def chunk(n, carry):
        low, high, start_max, slot_min = (bounds[16 * v + n, 0] for v in range(4))

        @pl.when(high >= 0)
        def _():
            rows = pl.ds(pl.multiple_of(n * CHUNK, CHUNK), CHUNK)
            queries = jnp.concatenate(
                [qsort[rows, h * HS:(h + 1) * HS] for h in range(HQ)], axis=0)
            half = lanes[pl.ds(n, 1), :]
            mine = jnp.concatenate([half, half], axis=1)
            half = lanes[pl.ds(n + 16, 1), :]
            begin = jnp.concatenate([half, half], axis=1)

            count = (high // ROWS - low // ROWS + 4) // 4
            first = jnp.maximum(high // ROWS + 1 - 4 * count, 0)
            origin = first * ROWS
            full_from = jnp.clip((start_max - origin + KT - 1) // KT - 1, 0, count - 1)
            full_to = jnp.clip((slot_min + 1 - origin) // KT - 1, full_from, count - 1)
            acc[...] = jnp.zeros_like(acc)

            def scores(masked, t):
                keys = k_v[pl.ds(first + 4 * t, 4)].reshape(KT, HS)
                s = scale * lax.dot_general(
                    keys, queries, (((1,), (1,)), ((), ())), preferred_element_type=F32)
                if masked:
                    at = lax.broadcasted_iota(jnp.int32, (KT, wide), 0)
                    base = origin + t * KT
                    s = jnp.where((at >= begin - base) & (at <= mine - base), s, -1e30)
                return s, jnp.max(s, axis=0, keepdims=True)

            def weigh(t, state):
                top, total, peak = state
                new = jnp.maximum(top, peak)
                p = jnp.exp2(s_a[...] - new)
                factor = jnp.exp2(top - new)
                total = total * factor + jnp.sum(p, axis=0, keepdims=True)
                values = jnp.concatenate([vt_v[first + 4 * t + u] for u in range(4)], axis=1)
                acc[...] = acc[...] * factor + jnp.dot(
                    values, p.astype(BF), preferred_element_type=F32)
                return new, total

            def tile(masked, t, state):
                s, peak = scores(masked, t + 1)
                new, total = weigh(t, state)
                s_a[...] = s
                return new, total, peak

            s, peak = scores(True, 0)
            s_a[...] = s
            state = (jnp.full((1, wide), -1e30, F32), jnp.zeros((1, wide), F32), peak)
            state = lax.fori_loop(0, full_from, functools.partial(tile, True), state)
            state = lax.fori_loop(full_from, full_to, functools.partial(tile, False), state)
            state = lax.fori_loop(full_to, count - 1, functools.partial(tile, True), state)
            top, total = weigh(count - 1, state)
            o = jnp.transpose(acc[...] / total).astype(BF)
            for h in range(HQ):
                osort[rows, h * HS:(h + 1) * HS] = o[h * CHUNK:(h + 1) * CHUNK, :]

        return carry

    lax.fori_loop(0, NCHUNK, chunk, 0)
    out[...] = jnp.dot(one[...], osort[...], preferred_element_type=F32).astype(BF)


def attend(bounds, lanes, qsort, one, kall, vtall):
    vmem = pl.BlockSpec(memory_space=pltpu.VMEM)
    smem = pl.BlockSpec(memory_space=pltpu.SMEM)
    wide = CHUNK * HQ
    return pl.pallas_call(
        attend_kernel,
        out_shape=jax.ShapeDtypeStruct((NPACK, HQ * HS), BF),
        in_specs=[smem, vmem, vmem, vmem, vmem, vmem],
        out_specs=vmem,
        scratch_shapes=[
            pltpu.VMEM((NPACK, HQ * HS), BF),
            pltpu.VMEM((KT, wide), F32),
            pltpu.VMEM((HS, wide), F32),
        ],
        compiler_params=pltpu.CompilerParams(vmem_limit_bytes=16 << 20),
        name="attend",
    )(bounds, lanes, qsort, one, kall, vtall)


def back_kernel(packed, ret, send_sem, recv_sem):
    x, y, z, c = place()
    line = z * 2 + c
    peers = []
    for dz in range(4):
        for dc in range(2):
            if (dz, dc) != (0, 0):
                peers.append(((z + dz) % 4, c if dc == 0 else 1 - c))
    barrier = pltpu.get_barrier_semaphore()
    for pz, pc in peers:
        pl.semaphore_signal(barrier, inc=1, device_id=device(x, y, pz, pc), device_id_type=MESH)
    pl.semaphore_wait(barrier, 7)
    for pz, pc in peers:
        pltpu.make_async_remote_copy(
            src_ref=packed.at[pl.ds((pz * 2 + pc) * PACK, PACK), :],
            dst_ref=ret.at[pl.ds(line * PACK, PACK), :],
            send_sem=send_sem.at[0], recv_sem=recv_sem.at[0],
            device_id=device(x, y, pz, pc), device_id_type=MESH).start()
    pltpu.make_async_copy(
        packed.at[pl.ds(line * PACK, PACK), :], ret.at[pl.ds(line * PACK, PACK), :], recv_sem.at[0]).start()
    pltpu.make_async_copy(ret, ret, recv_sem.at[0]).wait()
    part = packed.at[pl.ds(0, 7 * PACK), :]
    pltpu.make_async_copy(part, part, send_sem.at[0]).wait()


def back(packed):
    vmem = pl.BlockSpec(memory_space=pltpu.VMEM)
    return pl.pallas_call(
        back_kernel,
        out_shape=jax.ShapeDtypeStruct((NPACK, HQ * HS), BF),
        in_specs=[vmem],
        out_specs=pl.BlockSpec(memory_space=pl.ANY),
        scratch_shapes=[pltpu.SemaphoreType.DMA((1,)), pltpu.SemaphoreType.DMA((1,))],
        compiler_params=pltpu.CompilerParams(collective_id=1, has_side_effects=True, vmem_limit_bytes=4 << 20),
        name="back",
    )(packed)


def finish_kernel(pack, ret, out):
    out[...] = dot_t(pack[...], ret[...]).astype(BF)


def finish(pack, ret):
    vmem = pl.BlockSpec(memory_space=pltpu.VMEM)
    return pl.pallas_call(
        finish_kernel,
        out_shape=jax.ShapeDtypeStruct((ROWS, HQ * HS), BF),
        in_specs=[vmem, vmem],
        out_specs=vmem,
        compiler_params=pltpu.CompilerParams(vmem_limit_bytes=8 << 20),
        name="finish",
    )(pack, ret)


def shards(tokens, query_weight, key_weight, value_weight, doc_lengths, slot_index):
    frequency = 500000.0 ** (-(jnp.arange(HS // 2, dtype=F32) * 2.0 / HS))
    frequency = jnp.concatenate([frequency, frequency])[None, :]
    ints = jnp.concatenate([slot_index[None, :], jnp.pad(doc_lengths, ((0, 3), (0, ROWS - 4)))], axis=0)
    kall, vtall, qsort, one, lanes, bounds, pack = front(
        ints, frequency, tokens, query_weight, key_weight, value_weight)
    packed = attend(bounds, lanes, qsort, one, kall, vtall)
    return finish(pack, back(packed))


def solution(mesh):
    in_specs = (P(("seq", "blk"), None), P(), P(), P(), P(), P(("seq", "blk")))
    out_specs = P(("seq", "blk"), None)
    return jax.shard_map(shards, mesh=mesh, in_specs=in_specs, out_specs=out_specs, check_vma=False)
```

```python
import functools
import math

import jax
import jax.numpy as jnp
from jax import lax
from jax.experimental import pallas as pl
from jax.experimental.pallas import tpu as pltpu
from jax.sharding import PartitionSpec as P

HQ = 8
HS = 128
D = 8192
ROWS = 256
NBLOCKS = 32
CAP = 3
PACK = 48
NPACK = 8 * PACK
QW = 128 + HQ * HS
TILES = (3, 4, 5, 6, 8)
KPARTS = 8
CHUNK = 32
NCHUNK = NPACK // CHUNK
MESH = pl.DeviceIdType.MESH
BF = jnp.bfloat16
F32 = jnp.float32
HIGHEST = lax.Precision.HIGHEST


def place():
    seq = lax.axis_index("seq")
    blk = lax.axis_index("blk")
    core = seq % 2
    y = (blk // 4) % 2 * 2 + seq // 2
    return blk // 8, y, blk % 4, core


def device(x, y, z, c):
    return ((y % 2) * 2 + c, (x * 2 + y // 2) * 4 + z)


def block_id(x, y, c):
    return c * 16 + x * 4 + y


def dot_t(a, b):
    return lax.dot_general(a, b, (((0,), (0,)), ((), ())), preferred_element_type=F32)


def rope(v, cos, sin):
    return v * cos + pltpu.roll(v, HS // 2, 1) * sin


def front_kernel(
    ints, freq, tok, wq, wk, wv,
    kall, vtall, qsort, one_o, lanes_o, bounds_o, pack_o,
    lengths, cos, sin, tok_v, wkv_v, wq_v, acc, kvs, zin, perm, aout, ain, kblk, vblk, qs, qin,
    tok_sem, wq_sem, zs_sem, zr_sem, as_sem, ar_sem, qs_sem, qr_sem,
    ts_sem, tr_sem, dr_sem, loc_sem, small_sem,
):
    x, y, z, c = place()
    xs, ys, zs = ([v if n == 0 else (v + n) % 4 for n in range(4)] for v in (x, y, z))
    low, high = [v % 2 * 2 for v in ys], [v // 2 * 4 for v in ys]
    cs = [c, 1 - c]
    kc = D // KPARTS
    mine = block_id(x, y, c)

    def at(dx, dy, dz, dc):
        return low[dy] + cs[dc], xs[dx] * 8 + high[dy] + zs[dz]

    line = z * 2 + c

    small = pltpu.make_async_copy(ints, lengths, small_sem.at[0])
    small.start()
    loads = []
    for i in range(KPARTS):
        part = pl.ds(i * kc, kc)
        loads.append([
            pltpu.make_async_copy(tok.at[:, part], tok_v.at[:, part], tok_sem.at[0, i]),
            pltpu.make_async_copy(wk.at[part, :], wkv_v.at[part, pl.ds(0, HS)], tok_sem.at[1, i]),
            pltpu.make_async_copy(wv.at[part, :], wkv_v.at[part, pl.ds(HS, HS)], tok_sem.at[2, i]),
        ])
        for load in loads[i]:
            load.start()
    qloads = []
    for n in range(4):
        cols = pl.ds(n * 256, 256)
        qloads.append(pltpu.make_async_copy(wq.at[:, cols], wq_v.at[n], wq_sem.at[n]))

    peers = [(dz, dc) for dz in range(4) for dc in range(2)][1:]
    flat = [(dx, dy, dc) for dx in range(4) for dy in range(4) for dc in range(2)][1:]
    flat.sort(key=lambda o: -(min(o[0], 4 - o[0]) + min(o[1], 4 - o[1])))
    barrier = pltpu.get_barrier_semaphore()
    for dz, dc in peers:
        pl.semaphore_signal(barrier, inc=1, device_id=at(0, 0, dz, dc), device_id_type=MESH)
    for dx, dy, dc in flat:
        pl.semaphore_signal(barrier, inc=1, device_id=at(dx, dy, 0, dc), device_id_type=MESH)

    slot_r = ints[0:1, :]
    block_r = slot_r >> 8
    slot_c = jnp.transpose(jnp.broadcast_to(slot_r.astype(F32), (HS, ROWS))).astype(jnp.int32)
    block_c = slot_c >> 8
    block_w = jnp.concatenate([block_c, block_c], axis=1)
    earlier = lax.broadcasted_iota(jnp.int32, (ROWS, ROWS), 0) < lax.broadcasted_iota(jnp.int32, (ROWS, ROWS), 1)
    rank_r = jnp.sum(
        ((block_w == block_r) & earlier).astype(F32), axis=0, keepdims=True).astype(jnp.int32)
    pidx = (block_r >> 5) * 96 + (block_r & 1) * PACK + ((block_r & 31) >> 1) * CAP + rank_r
    lane = lax.broadcasted_iota(jnp.int32, (NPACK, ROWS), 0)
    pack = (lane == pidx).astype(F32).astype(BF)
    pack_o[...] = pack
    meta = ((slot_c & 255) + 1).astype(F32).astype(BF)
    slots = jnp.dot(pack, meta, preferred_element_type=F32).astype(BF)
    kvs[:, 2 * HS:] = slots
    qs[:, 0:128] = slots
    small.wait()
    local_c = slot_c & 8191
    group_c = slot_c >> 13
    start_c = jnp.zeros_like(slot_c)
    for g in range(4):
        end = 0
        for d in range(3):
            end = end + lengths[1 + g, d]
            start_c = jnp.where((group_c == g) & (local_c >= end), end, start_c)
    angle = (local_c - start_c).astype(F32) * freq[...]
    left = lax.broadcasted_iota(jnp.int32, (HS, HS), 1) < HS // 2
    angle = jnp.where(left, angle[:HS], angle[HS:])
    cosine, sine = jnp.cos(angle), jnp.sin(angle)
    cosine_r, sine_r = pltpu.roll(cosine, HS // 2, 1), pltpu.roll(sine, HS // 2, 1)
    cos[0:HS, :] = jnp.where(left, cosine, cosine_r)
    cos[HS:, :] = jnp.where(left, cosine_r, cosine)
    sin[0:HS, :] = jnp.where(left, -sine, sine_r)
    sin[HS:, :] = jnp.where(left, -sine_r, sine)

    for i in range(KPARTS):
        part = pl.ds(i * kc, kc)
        for load in loads[i]:
            load.wait()
        product = jnp.dot(tok_v[:, part], wkv_v[part, :], preferred_element_type=F32)
        if i == 0:
            acc[...] = product
        else:
            acc[...] += product
    for load in qloads:
        load.start()
    k_rows = rope(acc[:, :HS], cos[...], sin[...]).astype(BF)
    v_rows = acc[:, HS:].astype(BF)
    kvs[:, 0:HS] = jnp.dot(pack, k_rows, preferred_element_type=F32).astype(BF)
    kvs[:, HS:2 * HS] = jnp.dot(pack, v_rows, preferred_element_type=F32).astype(BF)

    pl.semaphore_wait(barrier, 7 + 31)

    for dz in (2, 1, 3):
        pltpu.make_async_remote_copy(
            src_ref=kvs.at[pl.ds(zs[dz] * 96, 96), :], dst_ref=zin.at[pl.ds(z * 96, 96), :],
            send_sem=zs_sem.at[0], recv_sem=zr_sem.at[0],
            device_id=at(0, 0, dz, 0), device_id_type=MESH).start()
    pltpu.make_async_copy(
        kvs.at[pl.ds(z * 96, 96), :], zin.at[pl.ds(z * 96, 96), :], zr_sem.at[0]).start()

    columns = (pl.ds(0, 128), pl.ds(128, 512), pl.ds(640, 512))

    def query_send(part):
        cols = columns[part]
        for dz, dc in peers:
            pltpu.make_async_remote_copy(
                src_ref=qs.at[pl.ds((zs[dz] * 2 + cs[dc]) * PACK, PACK), cols],
                dst_ref=qin.at[pl.ds(line * PACK, PACK), cols],
                send_sem=qs_sem.at[part], recv_sem=qr_sem.at[part],
                device_id=at(0, 0, dz, dc), device_id_type=MESH).start()
        pltpu.make_async_copy(
            qs.at[pl.ds(line * PACK, PACK), cols], qin.at[pl.ds(line * PACK, PACK), cols],
            qr_sem.at[part]).start()

    def query_wait(part):
        cols = columns[part]
        pltpu.make_async_copy(qin.at[:, cols], qin.at[:, cols], qr_sem.at[part]).wait()

    def sent(ref, sem):
        pltpu.make_async_copy(ref, ref, sem).wait()

    query_send(0)

    row = lax.broadcasted_iota(jnp.int32, (512, NPACK), 0)
    col = lax.broadcasted_iota(jnp.int32, (512, NPACK), 1)
    j = row >> 4
    slot12 = row & 15
    zz = (slot12 >= 3).astype(jnp.int32) + (slot12 >= 6).astype(jnp.int32) + (slot12 >= 9).astype(jnp.int32)
    source = zz * 96 + (j & 1) * 48 + (j >> 1) * 3 + (slot12 - 3 * zz)
    perm[...] = ((source == col) & (slot12 < 12)).astype(F32).astype(BF)

    def query_block(n):
        qloads[n].wait()
        acc[...] = jnp.zeros_like(acc)

        @pl.loop(0, 4)
        def _(i):
            part = pl.ds(pl.multiple_of(i * (D // 4), D // 4), D // 4)
            acc[...] += jnp.dot(tok_v[:, part], wq_v[n, part, :], preferred_element_type=F32)

        for h in range(2):
            rows = rope(acc[:, h * HS:(h + 1) * HS], cos[...], sin[...]).astype(BF)
            at = 128 + (n * 2 + h) * HS
            qs[:, at:at + HS] = jnp.dot(pack, rows, preferred_element_type=F32).astype(BF)

    query_block(0)

    pltpu.make_async_copy(zin, zin, zr_sem.at[0]).wait()
    aout[...] = jnp.dot(perm[...], zin[...], preferred_element_type=F32).astype(BF)
    for dx, dy, dc in flat:
        pltpu.make_async_remote_copy(
            src_ref=aout.at[pl.ds(block_id(xs[dx], ys[dy], cs[dc]) * 16, 16), :],
            dst_ref=ain.at[pl.ds(mine * 16, 16), :],
            send_sem=as_sem.at[0], recv_sem=ar_sem.at[0],
            device_id=at(dx, dy, 0, dc), device_id_type=MESH).start()
    pltpu.make_async_copy(
        aout.at[pl.ds(mine * 16, 16), :], ain.at[pl.ds(mine * 16, 16), :], ar_sem.at[0]).start()

    query_block(1)
    query_send(1)
    query_block(2)

    query_wait(0)
    shape = (NPACK, HS)
    i = lax.broadcasted_iota(jnp.int32, shape, 0)
    w = i - ((i * 43691) >> 21) * PACK
    base = ((w * 43691) >> 17) * 2 + c
    m = qin[:, 0:HS].astype(F32)
    slot = jnp.where(m > 0.0, base.astype(F32) * 256.0 + m - 1.0, -1.0 - i.astype(F32))
    slot_row = jnp.transpose(slot)[0:1, :]
    slot_wide = jnp.concatenate([slot] * 3, axis=1)
    rank = jnp.sum((slot_row < slot_wide).astype(F32), axis=1, keepdims=True)
    lane = lax.broadcasted_iota(jnp.int32, (NPACK, NPACK), 1).astype(F32)
    one_o[...] = (lane == rank).astype(F32).astype(BF)
    rank_wide = jnp.broadcast_to(rank, shape)
    lane_q = (lax.broadcasted_iota(jnp.int32, shape, 1) & (CHUNK - 1)).astype(F32)
    lanes_o[0:16, :] = jnp.full((16, HS), -1, jnp.int32)
    for n in range(NCHUNK):
        pick = rank_wide == lane_q + float(n * CHUNK)
        lanes_o[n:n + 1, :] = jnp.sum(
            jnp.where(pick, slot, 0.0), axis=0, keepdims=True).astype(jnp.int32)
    slots = lanes_o[0:16, :]
    start = jnp.zeros_like(slots)
    end = 0
    for d in range(3):
        end = end + lengths[1 + z, d]
        start = jnp.where(slots >= end, end, start)
    lanes_o[16:32, :] = start
    for n, v in enumerate((
        jnp.min(jnp.where(slots >= 0, start, 8192), axis=1, keepdims=True),
        jnp.max(slots, axis=1, keepdims=True),
        jnp.max(jnp.where(slots >= 0, start, 0), axis=1, keepdims=True),
        jnp.min(jnp.where(slots >= 0, slots, 8192), axis=1, keepdims=True),
    )):
        bounds_o[n * 16:(n + 1) * 16, :] = jnp.broadcast_to(v, (16, HS))

    query_block(3)
    query_send(2)

    pltpu.make_async_copy(ain, ain, ar_sem.at[0]).wait()
    got = ain[:, 2 * HS:].astype(F32)
    want = (lax.broadcasted_iota(jnp.int32, (512, HS), 1) + 1).astype(F32)
    one = jnp.concatenate([
        (got == want).astype(F32), (got == want + 128.0).astype(F32)], axis=1).astype(BF)
    kblk[...] = dot_t(one, ain[:, 0:HS]).astype(BF)
    vblk[...] = dot_t(ain[:, HS:2 * HS], one).astype(BF)

    blocks = [[
        (xs[a] + (xs[b] - xs[a]) * c) * 4 + ys[b] + (ys[a] - ys[b]) * c + 16 * c
        for b in range(4)] for a in range(4)]

    def along(a, b):
        one, two = at(a, b, 0, 0), at(b, a, 0, 0)
        return tuple(u + (v - u) * c for u, v in zip(one, two))

    first, second = [None] + [along(n, 0) for n in (1, 2, 3)], [None] + [along(0, n) for n in (1, 2, 3)]

    def piece(q, a, b):
        return (kall if q == 0 else vtall).at[blocks[a][b]]

    def source_of(q, a, b):
        if (a, b) == (0, 0):
            return kblk if q == 0 else vblk
        return piece(q, a, b)

    def push(q, a, b, da, db):
        pltpu.make_async_remote_copy(
            src_ref=source_of(q, a, b), dst_ref=piece(q, a, b),
            send_sem=ts_sem.at[q], recv_sem=tr_sem.at[q * 16 + (a - da) % 4 * 4 + (b - db) % 4],
            device_id=first[da] if db == 0 else second[db], device_id_type=MESH).start()

    partner = at(0, 0, 0, 1)

    def share(q, a, b):
        pltpu.make_async_remote_copy(
            src_ref=source_of(q, a, b), dst_ref=piece(q, a, b),
            send_sem=ts_sem.at[q], recv_sem=dr_sem.at[q],
            device_id=partner, device_id_type=MESH).start()

    local = [
        pltpu.make_async_copy(source_of(q, 0, 0), piece(q, 0, 0), loc_sem.at[q]) for q in range(2)]
    for da in (1, 3, 2):
        for q in range(2):
            push(q, 0, 0, da, 0)
    for db in (1, 3):
        for q in range(2):
            push(q, 0, 0, 0, db)
    for q in range(2):
        local[q].start()
        share(q, 0, 0)

    def arrive(q, a, b):
        ref = piece(q, a, b)
        pltpu.make_async_copy(ref, ref, tr_sem.at[q * 16 + a * 4 + b]).wait()
        if b == 0:
            push(q, a, b, 0, 1)
            push(q, a, b, 0, 3)
        elif b == (3, 1)[q]:
            push(q, a, b, 0, (1, 3)[q])
        share(q, a, b)

    for a, b in ((1, 0), (3, 0), (0, 1), (0, 3), (2, 0), (1, 1), (1, 3), (3, 1), (3, 3), (2, 1), (2, 3)):
        for q in range(2):
            arrive(q, a, b)
    query_wait(1)
    query_wait(2)
    qsort[...] = dot_t(one_o[...], qin[:, HS:]).astype(BF)
    sent(zin.at[pl.ds(0, 288), :], zs_sem.at[0])
    sent(aout.at[pl.ds(0, 31 * 16), :], as_sem.at[0])
    for n, cols in enumerate(columns):
        sent(qs.at[pl.ds(0, 7 * PACK), cols], qs_sem.at[n])
    for a, b in ((0, 2), (1, 2), (3, 2), (2, 2)):
        for q in range(2):
            arrive(q, a, b)
    other = pl.ds((1 - c) * 16, 16)
    pltpu.make_async_copy(kall.at[other], kall.at[other], dr_sem.at[0]).wait()
    pltpu.make_async_copy(vtall.at[other], vtall.at[other], dr_sem.at[1]).wait()
    for copy in local:
        copy.wait()
    sent(kall.at[pl.ds(0, 31)], ts_sem.at[0])
    sent(vtall.at[pl.ds(0, 31)], ts_sem.at[1])


def front(ints, freq, tokens, wq, wk, wv):
    anyspace = pl.BlockSpec(memory_space=pl.ANY)
    vmem = pl.BlockSpec(memory_space=pltpu.VMEM)
    dma = pltpu.SemaphoreType.DMA
    return pl.pallas_call(
        front_kernel,
        out_shape=(
            jax.ShapeDtypeStruct((NBLOCKS, ROWS, HS), BF),
            jax.ShapeDtypeStruct((NBLOCKS, HS, ROWS), BF),
            jax.ShapeDtypeStruct((NPACK, HQ * HS), BF),
            jax.ShapeDtypeStruct((NPACK, NPACK), BF),
            jax.ShapeDtypeStruct((32, HS), jnp.int32),
            jax.ShapeDtypeStruct((64, HS), jnp.int32),
            jax.ShapeDtypeStruct((NPACK, ROWS), BF),
        ),
        in_specs=[vmem, vmem] + [anyspace] * 4,
        out_specs=(anyspace, anyspace, vmem, vmem, vmem, vmem, vmem),
        scratch_shapes=[
            pltpu.SMEM((8, ROWS), jnp.int32),
            pltpu.VMEM((ROWS, HS), F32),
            pltpu.VMEM((ROWS, HS), F32),
            pltpu.VMEM((ROWS, D), BF),
            pltpu.VMEM((D, 2 * HS), BF),
            pltpu.VMEM((4, D, 256), BF),
            pltpu.VMEM((ROWS, 256), F32),
            pltpu.VMEM((NPACK, 3 * HS), BF),
            pltpu.VMEM((NPACK, 3 * HS), BF),
            pltpu.VMEM((512, NPACK), BF),
            pltpu.VMEM((512, 3 * HS), BF),
            pltpu.VMEM((512, 3 * HS), BF),
            pltpu.VMEM((ROWS, HS), BF),
            pltpu.VMEM((HS, ROWS), BF),
            pltpu.VMEM((NPACK, QW), BF),
            pltpu.VMEM((NPACK, QW), BF),
            dma((3, KPARTS)), dma((4,)), dma((1,)), dma((1,)), dma((1,)), dma((1,)),
            dma((3,)), dma((3,)), dma((2,)), dma((32,)), dma((2,)), dma((2,)), dma((1,)),
        ],
        compiler_params=pltpu.CompilerParams(
            collective_id=0, has_side_effects=True, vmem_limit_bytes=47 << 20),
        name="front",
    )(ints, freq, tokens, wq, wk, wv)


def attend_kernel(
    bounds, lanes, qsort, one, k_v, vt_v, out, osort, s_a, acc, total_s,
):
    osort[...] = jnp.zeros_like(osort)
    scale = math.log2(math.e) / math.sqrt(HS)
    wide = CHUNK * HQ

    def chunk(n, carry):
        low, high = bounds[n, 0], bounds[16 + n, 0]

        @pl.when(high >= 0)
        def _():
            rows = pl.ds(pl.multiple_of(n * CHUNK, CHUNK), CHUNK)
            queries = jnp.concatenate(
                [qsort[rows, h * HS:(h + 1) * HS] for h in range(HQ)], axis=0)
            half = lanes[pl.ds(n, 1), :]
            mine = jnp.concatenate([half, half], axis=1)
            half = lanes[pl.ds(n + 16, 1), :]
            begin = jnp.concatenate([half, half], axis=1)

            spans = high // ROWS - low // ROWS + 1
            counts = [(spans + nb - 1) // nb for nb in TILES]
            prices = [
                jnp.where(n * nb <= NBLOCKS, n * (174 + 62 * nb), 1 << 20)
                for n, nb in zip(counts, TILES)]
            best = functools.reduce(jnp.minimum, prices)
            acc[...] = jnp.zeros_like(acc)

            def run(nb, count):
                kt = nb * ROWS
                first = jnp.maximum(high // ROWS + 1 - nb * count, 0)
                origin = first * ROWS
                part = s_a.at[pl.ds(0, kt), :]

                def scores(t):
                    keys = k_v[pl.ds(first + nb * t, nb)].reshape(kt, HS)
                    s = scale * lax.dot_general(
                        keys, queries, (((1,), (1,)), ((), ())), preferred_element_type=F32)
                    at = lax.broadcasted_iota(jnp.int32, (kt, wide), 0)
                    base = origin + t * kt
                    past = (at - (begin - base)).astype(jnp.uint32)
                    s = jnp.where(past <= (mine - begin).astype(jnp.uint32), s, -1e30)
                    return s, jnp.max(s, axis=0, keepdims=True)

                def weigh(t, state):
                    top, total, peak = state
                    new = jnp.maximum(top, peak)
                    p = jnp.exp2(part[...] - new)
                    factor = jnp.exp2(top - new)
                    total = total * factor + jnp.sum(p, axis=0, keepdims=True)
                    values = jnp.concatenate([vt_v[first + nb * t + u] for u in range(nb)], axis=1)
                    acc[...] = acc[...] * factor + jnp.dot(
                        values, p.astype(BF), preferred_element_type=F32)
                    return new, total

                def tile(t, state):
                    s, peak = scores(t + 1)
                    new, total = weigh(t, state)
                    part[...] = s
                    return new, total, peak

                s, peak = scores(0)
                part[...] = s
                state = (jnp.full((1, wide), -1e30, F32), jnp.zeros((1, wide), F32), peak)
                state = lax.fori_loop(0, count - 1, tile, state)
                total_s[...] = weigh(count - 1, state)[1]

            taken = False
            for nb, count, price in zip(TILES, counts, prices):
                now = price == best
                pl.when(jnp.logical_and(now, jnp.logical_not(taken)))(functools.partial(run, nb, count))
                taken = jnp.logical_or(taken, now)
            total = total_s[...]
            o = jnp.transpose(acc[...] / total).astype(BF)
            for h in range(HQ):
                osort[rows, h * HS:(h + 1) * HS] = o[h * CHUNK:(h + 1) * CHUNK, :]

        return carry

    lax.fori_loop(0, NCHUNK, chunk, 0)
    out[...] = jnp.dot(one[...], osort[...], preferred_element_type=F32).astype(BF)


def attend(bounds, lanes, qsort, one, kall, vtall):
    vmem = pl.BlockSpec(memory_space=pltpu.VMEM)
    smem = pl.BlockSpec(memory_space=pltpu.SMEM)
    wide = CHUNK * HQ
    return pl.pallas_call(
        attend_kernel,
        out_shape=jax.ShapeDtypeStruct((NPACK, HQ * HS), BF),
        in_specs=[smem, vmem, vmem, vmem, vmem, vmem],
        out_specs=vmem,
        scratch_shapes=[
            pltpu.VMEM((NPACK, HQ * HS), BF),
            pltpu.VMEM((TILES[-1] * ROWS, wide), F32),
            pltpu.VMEM((HS, wide), F32),
            pltpu.VMEM((1, wide), F32),
        ],
        compiler_params=pltpu.CompilerParams(vmem_limit_bytes=16 << 20),
        name="attend",
    )(bounds, lanes, qsort, one, kall, vtall)


def back_kernel(packed, ret, send_sem, recv_sem):
    x, y, z, c = place()
    line = z * 2 + c
    peers = []
    for dz in range(4):
        for dc in range(2):
            if (dz, dc) != (0, 0):
                peers.append(((z + dz) % 4, c if dc == 0 else 1 - c))
    barrier = pltpu.get_barrier_semaphore()
    for pz, pc in peers:
        pl.semaphore_signal(barrier, inc=1, device_id=device(x, y, pz, pc), device_id_type=MESH)
    pl.semaphore_wait(barrier, 7)
    for pz, pc in peers:
        pltpu.make_async_remote_copy(
            src_ref=packed.at[pl.ds((pz * 2 + pc) * PACK, PACK), :],
            dst_ref=ret.at[pl.ds(line * PACK, PACK), :],
            send_sem=send_sem.at[0], recv_sem=recv_sem.at[0],
            device_id=device(x, y, pz, pc), device_id_type=MESH).start()
    pltpu.make_async_copy(
        packed.at[pl.ds(line * PACK, PACK), :], ret.at[pl.ds(line * PACK, PACK), :], recv_sem.at[0]).start()
    pltpu.make_async_copy(ret, ret, recv_sem.at[0]).wait()
    part = packed.at[pl.ds(0, 7 * PACK), :]
    pltpu.make_async_copy(part, part, send_sem.at[0]).wait()


def back(packed):
    vmem = pl.BlockSpec(memory_space=pltpu.VMEM)
    return pl.pallas_call(
        back_kernel,
        out_shape=jax.ShapeDtypeStruct((NPACK, HQ * HS), BF),
        in_specs=[vmem],
        out_specs=pl.BlockSpec(memory_space=pl.ANY),
        scratch_shapes=[pltpu.SemaphoreType.DMA((1,)), pltpu.SemaphoreType.DMA((1,))],
        compiler_params=pltpu.CompilerParams(collective_id=1, has_side_effects=True, vmem_limit_bytes=4 << 20),
        name="back",
    )(packed)


def finish_kernel(pack, ret, out):
    out[...] = dot_t(pack[...], ret[...]).astype(BF)


def finish(pack, ret):
    vmem = pl.BlockSpec(memory_space=pltpu.VMEM)
    return pl.pallas_call(
        finish_kernel,
        out_shape=jax.ShapeDtypeStruct((ROWS, HQ * HS), BF),
        in_specs=[vmem, vmem],
        out_specs=vmem,
        compiler_params=pltpu.CompilerParams(vmem_limit_bytes=8 << 20),
        name="finish",
    )(pack, ret)


def shards(tokens, query_weight, key_weight, value_weight, doc_lengths, slot_index):
    frequency = 500000.0 ** (-(jnp.arange(HS // 2, dtype=F32) * 2.0 / HS))
    frequency = jnp.concatenate([frequency, frequency])[None, :]
    ints = jnp.concatenate([slot_index[None, :], jnp.pad(doc_lengths, ((0, 3), (0, ROWS - 4)))], axis=0)
    kall, vtall, qsort, one, lanes, bounds, pack = front(
        ints, frequency, tokens, query_weight, key_weight, value_weight)
    packed = attend(bounds, lanes, qsort, one, kall, vtall)
    return finish(pack, back(packed))


def solution(mesh):
    in_specs = (P(("seq", "blk"), None), P(), P(), P(), P(), P(("seq", "blk")))
    out_specs = P(("seq", "blk"), None)
    return jax.shard_map(shards, mesh=mesh, in_specs=in_specs, out_specs=out_specs, check_vma=False)
```

```python
import functools
import math

import jax
import jax.numpy as jnp
from jax import lax
from jax.experimental import pallas as pl
from jax.experimental.pallas import tpu as pltpu
from jax.sharding import PartitionSpec as P

HQ = 8
HS = 128
D = 8192
ROWS = 256
NBLOCKS = 32
CAP = 3
PACK = 48
NPACK = 8 * PACK
QW = 128 + HQ * HS
KT = 1024
KPARTS = 8
CHUNK = 32
NCHUNK = NPACK // CHUNK
MESH = pl.DeviceIdType.MESH
BF = jnp.bfloat16
F32 = jnp.float32
HIGHEST = lax.Precision.HIGHEST


def place():
    seq = lax.axis_index("seq")
    blk = lax.axis_index("blk")
    core = seq % 2
    y = (blk // 4) % 2 * 2 + seq // 2
    return blk // 8, y, blk % 4, core


def device(x, y, z, c):
    return ((y % 2) * 2 + c, (x * 2 + y // 2) * 4 + z)


def block_id(x, y, c):
    return c * 16 + x * 4 + y


def dot_t(a, b):
    return lax.dot_general(a, b, (((0,), (0,)), ((), ())), preferred_element_type=F32)


def rope(v, cos, sin):
    return v * cos + pltpu.roll(v, HS // 2, 1) * sin


def front_kernel(
    ints, freq, tok, wq, wk, wv,
    kall, vtall, qsort, one_o, lanes_o, bounds_o, pack_o,
    lengths, cos, sin, tok_v, wkv_v, wq_v, acc, kvs, zin, perm, aout, ain, kblk, vblk, qs, qin,
    tok_sem, wq_sem, zs_sem, zr_sem, as_sem, ar_sem, qs_sem, qr_sem,
    ts_sem, tr_sem, dr_sem, loc_sem, small_sem,
):
    x, y, z, c = place()
    xs, ys, zs = ([v if n == 0 else (v + n) % 4 for n in range(4)] for v in (x, y, z))
    low, high = [v % 2 * 2 for v in ys], [v // 2 * 4 for v in ys]
    cs = [c, 1 - c]
    kc = D // KPARTS
    mine = block_id(x, y, c)

    def at(dx, dy, dz, dc):
        return low[dy] + cs[dc], xs[dx] * 8 + high[dy] + zs[dz]

    line = z * 2 + c

    small = pltpu.make_async_copy(ints, lengths, small_sem.at[0])
    small.start()
    loads = []
    for i in range(KPARTS):
        part = pl.ds(i * kc, kc)
        loads.append([
            pltpu.make_async_copy(tok.at[:, part], tok_v.at[:, part], tok_sem.at[0, i]),
            pltpu.make_async_copy(wk.at[part, :], wkv_v.at[part, pl.ds(0, HS)], tok_sem.at[1, i]),
            pltpu.make_async_copy(wv.at[part, :], wkv_v.at[part, pl.ds(HS, HS)], tok_sem.at[2, i]),
        ])
        for load in loads[i]:
            load.start()
    qloads = []
    for n in range(4):
        cols = pl.ds(n * 256, 256)
        qloads.append(pltpu.make_async_copy(wq.at[:, cols], wq_v.at[n], wq_sem.at[n]))

    peers = [(dz, dc) for dz in range(4) for dc in range(2)][1:]
    flat = [(dx, dy, dc) for dx in range(4) for dy in range(4) for dc in range(2)][1:]
    barrier = pltpu.get_barrier_semaphore()
    for dz, dc in peers:
        pl.semaphore_signal(barrier, inc=1, device_id=at(0, 0, dz, dc), device_id_type=MESH)
    for dx, dy, dc in flat:
        pl.semaphore_signal(barrier, inc=1, device_id=at(dx, dy, 0, dc), device_id_type=MESH)

    slot_r = ints[0:1, :]
    block_r = slot_r >> 8
    slot_c = jnp.transpose(jnp.broadcast_to(slot_r.astype(F32), (HS, ROWS))).astype(jnp.int32)
    block_c = slot_c >> 8
    block_w = jnp.concatenate([block_c, block_c], axis=1)
    earlier = lax.broadcasted_iota(jnp.int32, (ROWS, ROWS), 0) < lax.broadcasted_iota(jnp.int32, (ROWS, ROWS), 1)
    rank_r = jnp.sum(
        ((block_w == block_r) & earlier).astype(F32), axis=0, keepdims=True).astype(jnp.int32)
    pidx = (block_r >> 5) * 96 + (block_r & 1) * PACK + ((block_r & 31) >> 1) * CAP + rank_r
    lane = lax.broadcasted_iota(jnp.int32, (NPACK, ROWS), 0)
    pack = (lane == pidx).astype(F32).astype(BF)
    pack_o[...] = pack
    meta = ((slot_c & 255) + 1).astype(F32).astype(BF)
    slots = jnp.dot(pack, meta, preferred_element_type=F32).astype(BF)
    kvs[:, 2 * HS:] = slots
    qs[:, 0:128] = slots
    small.wait()
    local_c = slot_c & 8191
    group_c = slot_c >> 13
    start_c = jnp.zeros_like(slot_c)
    for g in range(4):
        end = 0
        for d in range(3):
            end = end + lengths[1 + g, d]
            start_c = jnp.where((group_c == g) & (local_c >= end), end, start_c)
    angle = (local_c - start_c).astype(F32) * freq[...]
    left = lax.broadcasted_iota(jnp.int32, (HS, HS), 1) < HS // 2
    angle = jnp.where(left, angle[:HS], angle[HS:])
    cosine, sine = jnp.cos(angle), jnp.sin(angle)
    cosine_r, sine_r = pltpu.roll(cosine, HS // 2, 1), pltpu.roll(sine, HS // 2, 1)
    cos[0:HS, :] = jnp.where(left, cosine, cosine_r)
    cos[HS:, :] = jnp.where(left, cosine_r, cosine)
    sin[0:HS, :] = jnp.where(left, -sine, sine_r)
    sin[HS:, :] = jnp.where(left, -sine_r, sine)

    for i in range(KPARTS):
        part = pl.ds(i * kc, kc)
        for load in loads[i]:
            load.wait()
        product = jnp.dot(tok_v[:, part], wkv_v[part, :], preferred_element_type=F32)
        if i == 0:
            acc[...] = product
        else:
            acc[...] += product
    for load in qloads:
        load.start()
    k_rows = rope(acc[:, :HS], cos[...], sin[...]).astype(BF)
    v_rows = acc[:, HS:].astype(BF)
    kvs[:, 0:HS] = jnp.dot(pack, k_rows, preferred_element_type=F32).astype(BF)
    kvs[:, HS:2 * HS] = jnp.dot(pack, v_rows, preferred_element_type=F32).astype(BF)

    pl.semaphore_wait(barrier, 7 + 31)

    for dz in range(1, 4):
        pltpu.make_async_remote_copy(
            src_ref=kvs.at[pl.ds(zs[dz] * 96, 96), :], dst_ref=zin.at[pl.ds(z * 96, 96), :],
            send_sem=zs_sem.at[0], recv_sem=zr_sem.at[0],
            device_id=at(0, 0, dz, 0), device_id_type=MESH).start()
    pltpu.make_async_copy(
        kvs.at[pl.ds(z * 96, 96), :], zin.at[pl.ds(z * 96, 96), :], zr_sem.at[0]).start()

    columns = (pl.ds(0, 128), pl.ds(128, 512), pl.ds(640, 512))

    def query_send(part):
        cols = columns[part]
        for dz, dc in peers:
            pltpu.make_async_remote_copy(
                src_ref=qs.at[pl.ds((zs[dz] * 2 + cs[dc]) * PACK, PACK), cols],
                dst_ref=qin.at[pl.ds(line * PACK, PACK), cols],
                send_sem=qs_sem.at[part], recv_sem=qr_sem.at[part],
                device_id=at(0, 0, dz, dc), device_id_type=MESH).start()
        pltpu.make_async_copy(
            qs.at[pl.ds(line * PACK, PACK), cols], qin.at[pl.ds(line * PACK, PACK), cols],
            qr_sem.at[part]).start()

    def query_wait(part):
        cols = columns[part]
        pltpu.make_async_copy(qin.at[:, cols], qin.at[:, cols], qr_sem.at[part]).wait()

    def sent(ref, sem):
        pltpu.make_async_copy(ref, ref, sem).wait()

    query_send(0)

    row = lax.broadcasted_iota(jnp.int32, (512, NPACK), 0)
    col = lax.broadcasted_iota(jnp.int32, (512, NPACK), 1)
    j = row >> 4
    slot12 = row & 15
    zz = (slot12 >= 3).astype(jnp.int32) + (slot12 >= 6).astype(jnp.int32) + (slot12 >= 9).astype(jnp.int32)
    source = zz * 96 + (j & 1) * 48 + (j >> 1) * 3 + (slot12 - 3 * zz)
    perm[...] = ((source == col) & (slot12 < 12)).astype(F32).astype(BF)

    def query_block(n):
        qloads[n].wait()
        acc[...] = jnp.zeros_like(acc)

        @pl.loop(0, 4)
        def _(i):
            part = pl.ds(pl.multiple_of(i * (D // 4), D // 4), D // 4)
            acc[...] += jnp.dot(tok_v[:, part], wq_v[n, part, :], preferred_element_type=F32)

        for h in range(2):
            rows = rope(acc[:, h * HS:(h + 1) * HS], cos[...], sin[...]).astype(BF)
            at = 128 + (n * 2 + h) * HS
            qs[:, at:at + HS] = jnp.dot(pack, rows, preferred_element_type=F32).astype(BF)

    query_block(0)

    pltpu.make_async_copy(zin, zin, zr_sem.at[0]).wait()
    aout[...] = jnp.dot(perm[...], zin[...], preferred_element_type=F32).astype(BF)
    for dx, dy, dc in flat:
        pltpu.make_async_remote_copy(
            src_ref=aout.at[pl.ds(block_id(xs[dx], ys[dy], cs[dc]) * 16, 16), :],
            dst_ref=ain.at[pl.ds(mine * 16, 16), :],
            send_sem=as_sem.at[0], recv_sem=ar_sem.at[0],
            device_id=at(dx, dy, 0, dc), device_id_type=MESH).start()
    pltpu.make_async_copy(
        aout.at[pl.ds(mine * 16, 16), :], ain.at[pl.ds(mine * 16, 16), :], ar_sem.at[0]).start()

    query_block(1)
    query_send(1)
    query_block(2)

    query_wait(0)
    shape = (NPACK, HS)
    i = lax.broadcasted_iota(jnp.int32, shape, 0)
    w = i - ((i * 43691) >> 21) * PACK
    base = ((w * 43691) >> 17) * 2 + c
    m = qin[:, 0:HS].astype(F32)
    slot = jnp.where(m > 0.0, base.astype(F32) * 256.0 + m - 1.0, -1.0 - i.astype(F32))
    slot_row = jnp.transpose(slot)[0:1, :]
    slot_wide = jnp.concatenate([slot] * 3, axis=1)
    rank = jnp.sum((slot_row < slot_wide).astype(F32), axis=1, keepdims=True)
    lane = lax.broadcasted_iota(jnp.int32, (NPACK, NPACK), 1).astype(F32)
    one_o[...] = (lane == rank).astype(F32).astype(BF)
    rank_wide = jnp.broadcast_to(rank, shape)
    lane_q = (lax.broadcasted_iota(jnp.int32, shape, 1) & (CHUNK - 1)).astype(F32)
    lanes_o[0:16, :] = jnp.full((16, HS), -1, jnp.int32)
    for n in range(NCHUNK):
        pick = rank_wide == lane_q + float(n * CHUNK)
        lanes_o[n:n + 1, :] = jnp.sum(
            jnp.where(pick, slot, 0.0), axis=0, keepdims=True).astype(jnp.int32)
    slots = lanes_o[0:16, :]
    start = jnp.zeros_like(slots)
    end = 0
    for d in range(3):
        end = end + lengths[1 + z, d]
        start = jnp.where(slots >= end, end, start)
    lanes_o[16:32, :] = start
    for n, v in enumerate((
        jnp.min(jnp.where(slots >= 0, start, 8192), axis=1, keepdims=True),
        jnp.max(slots, axis=1, keepdims=True),
        jnp.max(jnp.where(slots >= 0, start, 0), axis=1, keepdims=True),
        jnp.min(jnp.where(slots >= 0, slots, 8192), axis=1, keepdims=True),
    )):
        bounds_o[n * 16:(n + 1) * 16, :] = jnp.broadcast_to(v, (16, HS))

    query_block(3)
    query_send(2)

    pltpu.make_async_copy(ain, ain, ar_sem.at[0]).wait()
    got = ain[:, 2 * HS:].astype(F32)
    want = (lax.broadcasted_iota(jnp.int32, (512, HS), 1) + 1).astype(F32)
    one = jnp.concatenate([
        (got == want).astype(F32), (got == want + 128.0).astype(F32)], axis=1).astype(BF)
    kblk[...] = dot_t(one, ain[:, 0:HS]).astype(BF)
    vblk[...] = dot_t(ain[:, HS:2 * HS], one).astype(BF)

    blocks = [[
        (xs[a] + (xs[b] - xs[a]) * c) * 4 + ys[b] + (ys[a] - ys[b]) * c + 16 * c
        for b in range(4)] for a in range(4)]

    def along(a, b):
        one, two = at(a, b, 0, 0), at(b, a, 0, 0)
        return tuple(u + (v - u) * c for u, v in zip(one, two))

    first, second = [None] + [along(n, 0) for n in (1, 2, 3)], [None] + [along(0, n) for n in (1, 2, 3)]

    def piece(q, a, b):
        return (kall if q == 0 else vtall).at[blocks[a][b]]

    def source_of(q, a, b):
        if (a, b) == (0, 0):
            return kblk if q == 0 else vblk
        return piece(q, a, b)

    def push(q, a, b, da, db):
        pltpu.make_async_remote_copy(
            src_ref=source_of(q, a, b), dst_ref=piece(q, a, b),
            send_sem=ts_sem.at[q], recv_sem=tr_sem.at[q * 16 + (a - da) % 4 * 4 + (b - db) % 4],
            device_id=first[da] if db == 0 else second[db], device_id_type=MESH).start()

    partner = at(0, 0, 0, 1)

    def share(q, a, b):
        pltpu.make_async_remote_copy(
            src_ref=source_of(q, a, b), dst_ref=piece(q, a, b),
            send_sem=ts_sem.at[q], recv_sem=dr_sem.at[q],
            device_id=partner, device_id_type=MESH).start()

    local = [
        pltpu.make_async_copy(source_of(q, 0, 0), piece(q, 0, 0), loc_sem.at[q]) for q in range(2)]
    for da in (1, 3, 2):
        for q in range(2):
            push(q, 0, 0, da, 0)
    for db in (1, 3):
        for q in range(2):
            push(q, 0, 0, 0, db)
    for q in range(2):
        local[q].start()
        share(q, 0, 0)

    def arrive(q, a, b):
        ref = piece(q, a, b)
        pltpu.make_async_copy(ref, ref, tr_sem.at[q * 16 + a * 4 + b]).wait()
        if b == 0:
            push(q, a, b, 0, 1)
            push(q, a, b, 0, 3)
        elif b == (3, 1)[q]:
            push(q, a, b, 0, (1, 3)[q])
        share(q, a, b)

    for a, b in ((1, 0), (3, 0), (0, 1), (0, 3), (2, 0), (1, 1), (1, 3), (3, 1), (3, 3), (2, 1), (2, 3)):
        for q in range(2):
            arrive(q, a, b)
    query_wait(1)
    query_wait(2)
    qsort[...] = dot_t(one_o[...], qin[:, HS:]).astype(BF)
    sent(zin.at[pl.ds(0, 288), :], zs_sem.at[0])
    sent(aout.at[pl.ds(0, 31 * 16), :], as_sem.at[0])
    for n, cols in enumerate(columns):
        sent(qs.at[pl.ds(0, 7 * PACK), cols], qs_sem.at[n])
    for a, b in ((0, 2), (1, 2), (3, 2), (2, 2)):
        for q in range(2):
            arrive(q, a, b)
    other = pl.ds((1 - c) * 16, 16)
    pltpu.make_async_copy(kall.at[other], kall.at[other], dr_sem.at[0]).wait()
    pltpu.make_async_copy(vtall.at[other], vtall.at[other], dr_sem.at[1]).wait()
    for copy in local:
        copy.wait()
    sent(kall.at[pl.ds(0, 31)], ts_sem.at[0])
    sent(vtall.at[pl.ds(0, 31)], ts_sem.at[1])


def front(ints, freq, tokens, wq, wk, wv):
    anyspace = pl.BlockSpec(memory_space=pl.ANY)
    vmem = pl.BlockSpec(memory_space=pltpu.VMEM)
    dma = pltpu.SemaphoreType.DMA
    return pl.pallas_call(
        front_kernel,
        out_shape=(
            jax.ShapeDtypeStruct((NBLOCKS, ROWS, HS), BF),
            jax.ShapeDtypeStruct((NBLOCKS, HS, ROWS), BF),
            jax.ShapeDtypeStruct((NPACK, HQ * HS), BF),
            jax.ShapeDtypeStruct((NPACK, NPACK), BF),
            jax.ShapeDtypeStruct((32, HS), jnp.int32),
            jax.ShapeDtypeStruct((64, HS), jnp.int32),
            jax.ShapeDtypeStruct((NPACK, ROWS), BF),
        ),
        in_specs=[vmem, vmem] + [anyspace] * 4,
        out_specs=(anyspace, anyspace, vmem, vmem, vmem, vmem, vmem),
        scratch_shapes=[
            pltpu.SMEM((8, ROWS), jnp.int32),
            pltpu.VMEM((ROWS, HS), F32),
            pltpu.VMEM((ROWS, HS), F32),
            pltpu.VMEM((ROWS, D), BF),
            pltpu.VMEM((D, 2 * HS), BF),
            pltpu.VMEM((4, D, 256), BF),
            pltpu.VMEM((ROWS, 256), F32),
            pltpu.VMEM((NPACK, 3 * HS), BF),
            pltpu.VMEM((NPACK, 3 * HS), BF),
            pltpu.VMEM((512, NPACK), BF),
            pltpu.VMEM((512, 3 * HS), BF),
            pltpu.VMEM((512, 3 * HS), BF),
            pltpu.VMEM((ROWS, HS), BF),
            pltpu.VMEM((HS, ROWS), BF),
            pltpu.VMEM((NPACK, QW), BF),
            pltpu.VMEM((NPACK, QW), BF),
            dma((3, KPARTS)), dma((4,)), dma((1,)), dma((1,)), dma((1,)), dma((1,)),
            dma((3,)), dma((3,)), dma((2,)), dma((32,)), dma((2,)), dma((2,)), dma((1,)),
        ],
        compiler_params=pltpu.CompilerParams(
            collective_id=0, has_side_effects=True, vmem_limit_bytes=47 << 20),
        name="front",
    )(ints, freq, tokens, wq, wk, wv)


def attend_kernel(
    bounds, lanes, qsort, one, k_v, vt_v, out, osort, s_a, acc,
):
    osort[...] = jnp.zeros_like(osort)
    scale = math.log2(math.e) / math.sqrt(HS)
    wide = CHUNK * HQ

    def chunk(n, carry):
        low, high, start_max, slot_min = (bounds[16 * v + n, 0] for v in range(4))

        @pl.when(high >= 0)
        def _():
            rows = pl.ds(pl.multiple_of(n * CHUNK, CHUNK), CHUNK)
            queries = jnp.concatenate(
                [qsort[rows, h * HS:(h + 1) * HS] for h in range(HQ)], axis=0)
            half = lanes[pl.ds(n, 1), :]
            mine = jnp.concatenate([half, half], axis=1)
            half = lanes[pl.ds(n + 16, 1), :]
            begin = jnp.concatenate([half, half], axis=1)

            count = (high // ROWS - low // ROWS + 4) // 4
            first = jnp.maximum(high // ROWS + 1 - 4 * count, 0)
            origin = first * ROWS
            full_from = jnp.clip((start_max - origin + KT - 1) // KT - 1, 0, count - 1)
            full_to = jnp.clip((slot_min + 1 - origin) // KT - 1, full_from, count - 1)
            acc[...] = jnp.zeros_like(acc)

            def scores(masked, t):
                keys = k_v[pl.ds(first + 4 * t, 4)].reshape(KT, HS)
                s = scale * lax.dot_general(
                    keys, queries, (((1,), (1,)), ((), ())), preferred_element_type=F32)
                if masked:
                    at = lax.broadcasted_iota(jnp.int32, (KT, wide), 0)
                    base = origin + t * KT
                    past = (at - (begin - base)).astype(jnp.uint32)
                    s = jnp.where(past <= (mine - begin).astype(jnp.uint32), s, -1e30)
                return s, jnp.max(s, axis=0, keepdims=True)

            def weigh(t, state):
                top, total, peak = state
                new = jnp.maximum(top, peak)
                p = jnp.exp2(s_a[...] - new)
                factor = jnp.exp2(top - new)
                total = total * factor + jnp.sum(p, axis=0, keepdims=True)
                values = jnp.concatenate([vt_v[first + 4 * t + u] for u in range(4)], axis=1)
                acc[...] = acc[...] * factor + jnp.dot(
                    values, p.astype(BF), preferred_element_type=F32)
                return new, total

            def tile(masked, t, state):
                s, peak = scores(masked, t + 1)
                new, total = weigh(t, state)
                s_a[...] = s
                return new, total, peak

            s, peak = scores(True, 0)
            s_a[...] = s
            state = (jnp.full((1, wide), -1e30, F32), jnp.zeros((1, wide), F32), peak)
            state = lax.fori_loop(0, full_from, functools.partial(tile, True), state)
            state = lax.fori_loop(full_from, full_to, functools.partial(tile, False), state)
            state = lax.fori_loop(full_to, count - 1, functools.partial(tile, True), state)
            top, total = weigh(count - 1, state)
            o = jnp.transpose(acc[...] / total).astype(BF)
            for h in range(HQ):
                osort[rows, h * HS:(h + 1) * HS] = o[h * CHUNK:(h + 1) * CHUNK, :]

        return carry

    lax.fori_loop(0, NCHUNK, chunk, 0)
    out[...] = jnp.dot(one[...], osort[...], preferred_element_type=F32).astype(BF)


def attend(bounds, lanes, qsort, one, kall, vtall):
    vmem = pl.BlockSpec(memory_space=pltpu.VMEM)
    smem = pl.BlockSpec(memory_space=pltpu.SMEM)
    wide = CHUNK * HQ
    return pl.pallas_call(
        attend_kernel,
        out_shape=jax.ShapeDtypeStruct((NPACK, HQ * HS), BF),
        in_specs=[smem, vmem, vmem, vmem, vmem, vmem],
        out_specs=vmem,
        scratch_shapes=[
            pltpu.VMEM((NPACK, HQ * HS), BF),
            pltpu.VMEM((KT, wide), F32),
            pltpu.VMEM((HS, wide), F32),
        ],
        compiler_params=pltpu.CompilerParams(vmem_limit_bytes=16 << 20),
        name="attend",
    )(bounds, lanes, qsort, one, kall, vtall)


def back_kernel(packed, ret, send_sem, recv_sem):
    x, y, z, c = place()
    line = z * 2 + c
    peers = []
    for dz in range(4):
        for dc in range(2):
            if (dz, dc) != (0, 0):
                peers.append(((z + dz) % 4, c if dc == 0 else 1 - c))
    barrier = pltpu.get_barrier_semaphore()
    for pz, pc in peers:
        pl.semaphore_signal(barrier, inc=1, device_id=device(x, y, pz, pc), device_id_type=MESH)
    pl.semaphore_wait(barrier, 7)
    for pz, pc in peers:
        pltpu.make_async_remote_copy(
            src_ref=packed.at[pl.ds((pz * 2 + pc) * PACK, PACK), :],
            dst_ref=ret.at[pl.ds(line * PACK, PACK), :],
            send_sem=send_sem.at[0], recv_sem=recv_sem.at[0],
            device_id=device(x, y, pz, pc), device_id_type=MESH).start()
    pltpu.make_async_copy(
        packed.at[pl.ds(line * PACK, PACK), :], ret.at[pl.ds(line * PACK, PACK), :], recv_sem.at[0]).start()
    pltpu.make_async_copy(ret, ret, recv_sem.at[0]).wait()
    part = packed.at[pl.ds(0, 7 * PACK), :]
    pltpu.make_async_copy(part, part, send_sem.at[0]).wait()


def back(packed):
    vmem = pl.BlockSpec(memory_space=pltpu.VMEM)
    return pl.pallas_call(
        back_kernel,
        out_shape=jax.ShapeDtypeStruct((NPACK, HQ * HS), BF),
        in_specs=[vmem],
        out_specs=pl.BlockSpec(memory_space=pl.ANY),
        scratch_shapes=[pltpu.SemaphoreType.DMA((1,)), pltpu.SemaphoreType.DMA((1,))],
        compiler_params=pltpu.CompilerParams(collective_id=1, has_side_effects=True, vmem_limit_bytes=4 << 20),
        name="back",
    )(packed)


def finish_kernel(pack, ret, out):
    out[...] = dot_t(pack[...], ret[...]).astype(BF)


def finish(pack, ret):
    vmem = pl.BlockSpec(memory_space=pltpu.VMEM)
    return pl.pallas_call(
        finish_kernel,
        out_shape=jax.ShapeDtypeStruct((ROWS, HQ * HS), BF),
        in_specs=[vmem, vmem],
        out_specs=vmem,
        compiler_params=pltpu.CompilerParams(vmem_limit_bytes=8 << 20),
        name="finish",
    )(pack, ret)


def shards(tokens, query_weight, key_weight, value_weight, doc_lengths, slot_index):
    frequency = 500000.0 ** (-(jnp.arange(HS // 2, dtype=F32) * 2.0 / HS))
    frequency = jnp.concatenate([frequency, frequency])[None, :]
    ints = jnp.concatenate([slot_index[None, :], jnp.pad(doc_lengths, ((0, 3), (0, ROWS - 4)))], axis=0)
    kall, vtall, qsort, one, lanes, bounds, pack = front(
        ints, frequency, tokens, query_weight, key_weight, value_weight)
    packed = attend(bounds, lanes, qsort, one, kall, vtall)
    return finish(pack, back(packed))


def solution(mesh):
    in_specs = (P(("seq", "blk"), None), P(), P(), P(), P(), P(("seq", "blk")))
    out_specs = P(("seq", "blk"), None)
    return jax.shard_map(shards, mesh=mesh, in_specs=in_specs, out_specs=out_specs, check_vma=False)
```
